512 devices in a mesh: ctx: 8 (over x, z_hi), ch: 64 (over z_lo, y, core).
Axes of the slice: x: 4, y: 4, z: 16 (z_hi: 2, z_lo: 8; z = z_hi * 8 + z_lo), core: 2. Of those that a mesh axis runs over, the one named last changes fastest.
Arguments:
- first_in: bfloat16 [2048, 65536], P('ch', 'ctx'), may hold values from -6 to 6
- second_in: bfloat16 [2048, 65536], P('ch', 'ctx'), may hold values from -6 to 6
- third_in: bfloat16 [2048, 65536], P('ch', 'ctx'), may hold values from -6 to 6
- grad_heads: bfloat16 [2048, 65536], P(None, ('ctx', 'ch')), may hold values from -6 to 6
- residue: float32 [128, 16], P('ch'), may hold values from -1.5 to 1.5
- decay_rate: float32 [128, 16], P('ch'), may hold values from 3.0517578e-06 to 0.1, as said below
- skip_gain: float32 [2048], P('ch'), may hold values from -3 to 3
Outputs:
- grad_first: bfloat16 [2048, 65536], P('ch', 'ctx')
- grad_second: bfloat16 [2048, 65536], P('ch', 'ctx')
- grad_third: bfloat16 [2048, 65536], P('ch', 'ctx')
- grad_residue: float32 [128, 16], P('ch')
- grad_skip: float32 [2048], P('ch')
The draws below stay inside these ranges and needn't reach their ends.
Inputs may be any that keep to these rules, and one draw needn't show every extreme that they name: `decay_rate`: positive decay rate of each mode.
All inputs are finite; a program needn't handle non-finite values.
Results may differ from the reference program's by a relative error of at most 0.006.
Values may be sent and summed in bfloat16 or wider, within the bound.
No kernel may reach another device: no remote copies, remote signals or barrier semaphores. Data moves between devices by JAX's collectives and lax.ppermute only.
A program may use at most 64 MiB of HBM per device.

```python
import jax
import jax.numpy as jnp
from jax import lax

GROUP = 16
NMODE = 16
CHANNELS = 2048
NGROUPS = 128
TOKENS = 65536


def draw_decay_rate(key, part):
    pick_key, slow_key, fast_key = jax.random.split(key, 3)
    slow_share = 0.5
    slow_pick = jax.random.uniform(pick_key, (NGROUPS, NMODE), jnp.float32) < slow_share
    slow_rate = jnp.exp(jax.random.uniform(slow_key, (NGROUPS, NMODE), jnp.float32, jnp.log(0.2 / TOKENS), jnp.log(2.0 / TOKENS)))
    fast_rate = jnp.exp(jax.random.uniform(fast_key, (NGROUPS, NMODE), jnp.float32, jnp.log(0.04), jnp.log(0.1)))
    return jnp.where(slow_pick, slow_rate, fast_rate)


def shard_levels(rng, dims, pieces, smallest, high):
    level, own = 1.0, jax.random.fold_in(rng, 6)
    for dim, blocks in pieces:
        draws = jnp.exp(jax.random.uniform(jax.random.fold_in(own, dim), (blocks,), jnp.float32, smallest / len(pieces), high / len(pieces)))
        level = level * jnp.repeat(draws, dims[dim] // blocks).reshape([-1 if axis == dim else 1 for axis in range(len(dims))])
    return level


def gaussian(stream_key, shape, spread, bound, shards=(), kind=jnp.bfloat16):
    drawn = jax.random.normal(stream_key, shape, jnp.float32) * spread
    if len(shards) > 0:
        drawn = shard_levels(stream_key, shape, shards, -0.22, 0.18) * drawn
    return jnp.clip(drawn, min=-bound, max=bound).astype(kind)


def setup_inputs(seed: int = 0) -> dict:
    arg_keys = jax.random.split(jax.random.key(seed), 8)
    first_in = gaussian(arg_keys[0], (CHANNELS, TOKENS), 1.0, 6.0, ((0, 64), (1, 8)))
    second_in = gaussian(arg_keys[1], (CHANNELS, TOKENS), 1.0, 6.0, ((0, 64), (1, 8)))
    third_in = gaussian(arg_keys[2], (CHANNELS, TOKENS), 1.0, 6.0, ((0, 64), (1, 8)))
    grad_heads = gaussian(arg_keys[3], (CHANNELS, TOKENS), 1.0, 6.0, ((1, 512),))
    residue = gaussian(arg_keys[4], (NGROUPS, NMODE), 0.25, 1.5, ((0, 64),), jnp.float32)
    decay_rate = draw_decay_rate(jax.random.fold_in(arg_keys[7], 71), 0)
    skip_gain = gaussian(arg_keys[6], (CHANNELS,), 0.5, 3.0, ((0, 64),), jnp.float32)
    return {"first_in": first_in, "second_in": second_in, "third_in": third_in, "grad_heads": grad_heads, "residue": residue, "decay_rate": decay_rate, "skip_gain": skip_gain}


def reference(first_in, second_in, third_in, grad_heads, residue, decay_rate, skip_gain):
    decay = jnp.repeat(jnp.exp(-decay_rate), GROUP, axis=0)
    weights = jnp.repeat(residue * jnp.sqrt(2.0 * decay_rate), GROUP, axis=0)
    gated = first_in.astype(jnp.float32) * second_in.astype(jnp.float32)
    grad_out = grad_heads.astype(jnp.float32)
    grad_conv = grad_out * third_in.astype(jnp.float32)
    zero_state = jnp.zeros(decay.shape, jnp.float32)

    def forward(carry, column):
        state, running = carry
        gated_t, grad_t = column
        state = decay * state + gated_t[:, None]
        running = running + grad_t[:, None] * state
        return ((state, running), lax.optimization_barrier(jnp.sum(weights * state, axis=1)) + skip_gain * gated_t)
    (final_state, totals), convolved = lax.scan(forward, (zero_state, zero_state), (gated.T, grad_conv.T))
    convolved = convolved.T

    def backward(state, grad_t):
        state = decay * state + grad_t[:, None]
        return (state, lax.optimization_barrier(jnp.sum(weights * state, axis=1)) + skip_gain * grad_t)
    first_state, grad_mixed = lax.scan(backward, zero_state, grad_conv.T, reverse=True)
    grad_mixed = grad_mixed.T
    grad_first = (grad_mixed * second_in.astype(jnp.float32)).astype(jnp.bfloat16)
    grad_second = (grad_mixed * first_in.astype(jnp.float32)).astype(jnp.bfloat16)
    grad_third = (grad_out * convolved).astype(jnp.bfloat16)
    grouped = lax.optimization_barrier(jnp.sum(totals.reshape(NGROUPS, GROUP, NMODE), axis=1))
    grad_residue = jnp.sqrt(2.0 * decay_rate) * grouped / jnp.sqrt(float(GROUP * TOKENS))
    grad_skip = lax.optimization_barrier(jnp.sum(grad_conv * gated, axis=1)) / jnp.sqrt(float(TOKENS))
    return (grad_first, grad_second, grad_third, grad_residue, grad_skip)
```

```python
import jax
import jax.numpy as jnp
from jax import lax
from jax.experimental import pallas as pl
from jax.experimental.pallas import tpu as pltpu
from jax.sharding import PartitionSpec as P

F32, BF16 = jnp.float32, jnp.bfloat16
SPAN = 128
SPANS = 64
GROUPS, WIDTH, MODES = 2, 16, 16
ROWS = SPANS * WIDTH
LENGTH = SPAN * SPANS
CTX = 8
TOKENS = LENGTH * CTX


def iota(shape, dim):
    return lax.broadcasted_iota(jnp.int32, shape, dim)


def high(x):
    return x.astype(BF16)


def low(x):
    return (x - x.astype(BF16).astype(F32)).astype(BF16)


def dot(a, b):
    return jnp.dot(a, b, preferred_element_type=F32)


def halves(x):
    return x[:, :128] + x[:, 128:]


def state_matrix(a_row, age):
    decay = jnp.exp(-a_row * age)
    lane_group = (iota((128, 128), 1) % 32) // MODES
    out = []
    for g in range(GROUPS):
        mine = jnp.where(lane_group == g, decay, 0.0)
        block = jnp.concatenate([high(mine), low(mine)], axis=1)
        out += [block, block]
    return jnp.concatenate(out, axis=0)


def mode_matrix(a_col, w_col, age):
    wave = w_col * jnp.exp(-a_col * age)
    row = iota((128, 128), 0)
    part = jnp.where(row < 64, wave.astype(BF16).astype(F32), low(wave).astype(F32))
    row_group = (row % 32) // MODES
    return jnp.concatenate(
        [jnp.where(row_group == g, part, 0.0).astype(BF16) for g in range(GROUPS)], axis=1
    )


def quad_split(x, lane):
    top = x.astype(BF16).astype(F32)
    return jnp.where((lane // 32) % 2 == 0, top, x - top).astype(BF16)


def toeplitz(a_s, w_s, g, gap):
    near = jnp.maximum(gap, 0).astype(F32)
    total = jnp.zeros((SPAN, SPAN), F32)
    for r in range(MODES):
        total = total + w_s[g, r] * jnp.exp(-a_s[g, r] * near)
    total = jnp.where(gap >= 0, total, 0.0)
    block = jnp.concatenate([high(total), low(total)], axis=1)
    return jnp.concatenate([block, block], axis=0)


def forward_kernel(
    first, second, a_row, a_col, w_col, a_s, w_s, skip,
    x_cat, x_turn, conv, enter, block_state, head_mat, near_mat, rise_j, back_toep, rise_mat, fall_mat, start_decay, later_decay,
    states, toep,
):
    a = a_row[...]
    row = iota((128, 128), 0)
    col = iota((128, 128), 1)
    token = row.astype(F32)
    lane_token = col.astype(F32)
    head_mat[...] = state_matrix(a, token + 1.0)
    near_mat[...] = state_matrix(a, token - 64.0)
    rise_j[...] = jnp.exp(a * (token - 64.0))
    rise_mat[...] = mode_matrix(a_col[...], w_col[...], lane_token)
    fall_mat[...] = mode_matrix(a_col[...], w_col[...], 127.0 - lane_token)
    n_row = iota((SPANS, 128), 0).astype(F32)
    start_decay[...] = jnp.exp(-a * (128.0 * n_row))
    later_decay[...] = jnp.exp(-a * (128.0 * (SPANS - 1.0 - n_row)))
    for g in range(GROUPS):
        toep[g] = toeplitz(a_s, w_s, g, col - row)
        back_toep[g] = toeplitz(a_s, w_s, g, row - col)
    for n in range(SPANS):
        at, here = pl.ds(n * WIDTH, WIDTH), pl.ds(n * SPAN, SPAN)
        x = first[:, here].astype(F32) * second[:, here].astype(F32)
        hi, lo = high(x), low(x)
        for g in range(GROUPS):
            c = slice(g * WIDTH, (g + 1) * WIDTH)
            x_cat[at, pl.ds(256 * g, 128)] = hi[c]
            x_cat[at, pl.ds(256 * g + 128, 128)] = lo[c]
    states[...] = halves(dot(x_cat[...], state_matrix(a, 128.0 - token)))
    step = jnp.exp(-a * 128.0)
    carry = jnp.zeros((WIDTH, 128), F32)
    for n in range(SPANS):
        at = pl.ds(n * WIDTH, WIDTH)
        enter[at, :] = carry
        carry = carry * step + states[at, :]
    block_state[...] = carry
    lane = iota((ROWS, 128), 1)
    conv[...] = dot(quad_split(enter[...], lane), rise_mat[...])
    for g in range(GROUPS):
        mine = pl.ds(256 * g, 256)
        here = pl.ds(128 * g, 128)
        x = x_cat[:, mine]
        gain = jnp.concatenate([skip[g]] * SPANS, axis=0)
        gated = x[:, :128].astype(F32) + x[:, 128:].astype(F32)
        conv[:, here] = conv[:, here] + halves(dot(x, toep[g])) + gain * gated
        x_turn[g] = x.T


def middle_kernel(
    grad_out, third, x_cat, x_turn, enter, block_state, head_mat, near_mat, rise_j, a_row,
    payload, g_cat, leave,
    states,
):
    a = a_row[...]
    total = jnp.zeros((GROUPS * WIDTH, SPAN), F32)
    for n in range(SPANS):
        at, here = pl.ds(n * WIDTH, WIDTH), pl.ds(n * SPAN, SPAN)
        y = grad_out[n].astype(F32) * third[:, here].astype(F32)
        hi, lo = high(y), low(y)
        x = []
        for g in range(GROUPS):
            c = slice(g * WIDTH, (g + 1) * WIDTH)
            g_cat[at, pl.ds(256 * g, 128)] = hi[c]
            g_cat[at, pl.ds(256 * g + 128, 128)] = lo[c]
            x.append(
                x_cat[at, pl.ds(256 * g, 128)].astype(F32)
                + x_cat[at, pl.ds(256 * g + 128, 128)].astype(F32)
            )
        total = total + y * jnp.concatenate(x, axis=0)
    states[...] = halves(dot(g_cat[...], head_mat[...]))
    row = iota((128, 128), 0)
    col = iota((128, 128), 1)
    cross = []
    for g in range(GROUPS):
        four = dot(x_turn[g], g_cat[:, pl.ds(256 * g, 256)])
        four = halves(four[:128] + four[128:])
        four = jnp.where(col >= row, four, 0.0)
        cross += [high(four), low(four)]
    near = halves(dot(jnp.concatenate(cross, axis=1), near_mat[...])) * rise_j[...]
    near = jnp.sum(near.reshape(16, 8, 128), axis=0)
    step = jnp.exp(-a * 128.0)
    carry = jnp.zeros((WIDTH, 128), F32)
    far = jnp.zeros((WIDTH, 128), F32)
    for n in reversed(range(SPANS)):
        at = pl.ds(n * WIDTH, WIDTH)
        leave[at, :] = carry
        now = states[at, :]
        far = far + now * enter[at, :]
        carry = carry * step + now
    weight = near + (far[:8] + far[8:]) * jnp.exp(a)
    direct = lax.dot_general(
        jnp.ones((8, SPAN), F32),
        jnp.concatenate([total] * 4, axis=0),
        (((1,), (1,)), ((), ())),
        precision=lax.Precision.HIGHEST,
        preferred_element_type=F32,
    )
    quarter = iota((8, 128), 1) // 32
    back = jnp.where(
        quarter == 0, carry[:8], jnp.where(quarter == 1, carry[8:], jnp.where(quarter == 2, weight, direct))
    )
    ahead = jnp.where(quarter == 0, block_state[:8, :], block_state[8:, :])
    for k in range(CTX):
        payload[k, :8, :] = back
        payload[k, 8:, :] = ahead


def backward_kernel(g_cat, leave, back_toep, fall_mat, skip, a_row, place, mixed, from_later, from_earlier):
    lane = iota((ROWS, 128), 1)
    mixed[...] = dot(quad_split(leave[...], lane), fall_mat[...])
    for g in range(GROUPS):
        here = pl.ds(128 * g, 128)
        y = g_cat[:, pl.ds(256 * g, 256)]
        gain = jnp.concatenate([skip[g]] * SPANS, axis=0)
        grad_conv = y[:, :128].astype(F32) + y[:, 128:].astype(F32)
        mixed[:, here] = mixed[:, here] + halves(dot(y, back_toep[g])) + gain * grad_conv
    a = jnp.broadcast_to(a_row[...], (8, 128)) * float(LENGTH)
    states = iota((8, 128), 1) < 64
    me = place[0]
    for k in range(CTX):
        after = jnp.maximum(k - me - 1, 0).astype(F32)
        before = jnp.maximum(me - 1 - k, 0).astype(F32)
        later = jnp.where(k > me, 1.0, 0.0)
        earlier = jnp.where(k < me, 1.0, 0.0)
        from_later[k] = jnp.where(states, jnp.exp(-a * after) * later, 1.0)
        from_earlier[k] = jnp.exp(-a * before) * earlier


def finish_kernel(
    parts, conv, mixed, grad_out, first, second, rise_mat, fall_mat, start_decay, later_decay, from_later, from_earlier, a_row,
    grad_first, grad_second, grad_third, grad_residue, grad_skip,
    left, result,
):
    a = a_row[...]
    quarter = iota((8, 128), 1) // 32
    back = jnp.zeros((8, 128), F32)
    ahead = jnp.zeros((8, 128), F32)
    running = jnp.zeros((8, 128), F32)
    far = jnp.zeros((8, 128), F32)
    block_step = jnp.exp(-a * float(LENGTH))
    for k in range(CTX):
        later, earlier = parts[k, :8, :], parts[k, 8:, :]
        back = back + later * from_later[k]
        ahead = ahead + earlier * from_earlier[k]
        far = far + later * running
        running = running * block_step + earlier

    def spread(x, q):
        x = jnp.where(quarter == q, x, 0.0)
        x = x + pltpu.roll(x, 32, 1)
        return x + pltpu.roll(x, 64, 1)

    def rows(x):
        return jnp.concatenate([spread(x, 0), spread(x, 1)], axis=0)

    lane = iota((ROWS, 128), 1)

    def fix(x, decay, matrix):
        whole = decay[...].reshape(SPANS, 1, 128) * x.reshape(1, WIDTH, 128)
        left[...] = quad_split(whole.reshape(ROWS, 128), lane)
        return dot(left[...], matrix[...])

    result[...] = conv[...] + fix(rows(ahead), start_decay, rise_mat)
    for n in range(SPANS):
        at, here = pl.ds(n * WIDTH, WIDTH), pl.ds(n * SPAN, SPAN)
        full = jnp.concatenate([result[at, pl.ds(0, 128)], result[at, pl.ds(128, 128)]], axis=0)
        grad_third[:, here] = (grad_out[n].astype(F32) * full).astype(BF16)
    result[...] = mixed[...] + fix(rows(back), later_decay, fall_mat)
    for n in range(SPANS):
        at, here = pl.ds(n * WIDTH, WIDTH), pl.ds(n * SPAN, SPAN)
        full = jnp.concatenate([result[at, pl.ds(0, 128)], result[at, pl.ds(128, 128)]], axis=0)
        grad_first[:, here] = (full * second[:, here].astype(F32)).astype(BF16)
        grad_second[:, here] = (full * first[:, here].astype(F32)).astype(BF16)
    near = spread(back, 2)
    crossed = (spread(far, 0) + spread(far, 1)) * jnp.exp(a)
    weight = jnp.sum(near + crossed, axis=0, keepdims=True)
    weight = weight * jnp.sqrt(2.0 * a) * (1.0 / (float(WIDTH * TOKENS) ** 0.5))
    grad_residue[0:1, :] = weight[:, :MODES]
    grad_residue[1:2, :] = pltpu.roll(weight, 128 - MODES, 1)[:, :MODES]
    direct = pltpu.roll(back, 32, 1)[0:1] * (1.0 / (float(TOKENS) ** 0.5))
    grad_skip[...] = direct[:, : GROUPS * WIDTH]


def call(kernel, outs, scratch, args, scalars=()):
    specs = [
        pl.BlockSpec(memory_space=pltpu.SMEM if i in scalars else pltpu.VMEM) for i in range(len(args))
    ]
    return pl.pallas_call(
        kernel,
        out_shape=tuple(jax.ShapeDtypeStruct(s, d) for s, d in outs),
        in_specs=specs,
        out_specs=tuple(pl.BlockSpec(memory_space=pltpu.VMEM) for _ in outs),
        scratch_shapes=[pltpu.VMEM(s, d) for s, d in scratch],
        compiler_params=pltpu.CompilerParams(vmem_limit_bytes=40 << 20),
    )(*args)


def prepare(residue, decay_rate, skip_gain):
    weight = residue * jnp.sqrt(2.0 * decay_rate)
    a_row = jnp.tile(decay_rate.reshape(1, 32), (1, 4))
    a_col = jnp.tile(decay_rate.reshape(32, 1), (4, 1))
    w_col = jnp.tile(weight.reshape(32, 1), (4, 1))
    return a_row, a_col, w_col, weight, skip_gain.reshape(GROUPS, WIDTH, 1)


def run_forward(first, second, a_row, a_col, w_col, a_s, w_s, skip):
    return call(
        forward_kernel,
        [
            ((ROWS, 512), BF16), ((GROUPS, 256, ROWS), BF16), ((ROWS, 256), F32), ((ROWS, 128), F32), ((WIDTH, 128), F32),
            ((512, 256), BF16), ((512, 256), BF16), ((128, 128), F32), ((GROUPS, 256, 256), BF16),
            ((128, 256), BF16), ((128, 256), BF16), ((SPANS, 128), F32), ((SPANS, 128), F32),
        ],
        [((ROWS, 128), F32), ((GROUPS, 256, 256), BF16)],
        (first, second, a_row, a_col, w_col, a_s, w_s, skip),
        scalars=(5, 6),
    )


def local(first, second, third, grad_out, exchange, residue, decay_rate, skip_gain, place):
    a_row, a_col, w_col, weight, skip = prepare(residue, decay_rate, skip_gain)
    (
        x_cat, x_turn, conv, enter, block_state, head_mat, near_mat, rise_j, back_toep,
        rise_mat, fall_mat, start_decay, later_decay,
    ) = run_forward(first, second, a_row, a_col, w_col, decay_rate, weight, skip)
    payload, g_cat, leave = call(
        middle_kernel,
        [((CTX, 16, 128), F32), ((ROWS, 512), BF16), ((ROWS, 128), F32)],
        [((ROWS, 128), F32)],
        (grad_out, third, x_cat, x_turn, enter, block_state, head_mat, near_mat, rise_j, a_row),
    )
    parts = exchange(payload)
    mixed, from_later, from_earlier = call(
        backward_kernel,
        [((ROWS, 256), F32), ((CTX, 8, 128), F32), ((CTX, 8, 128), F32)],
        [],
        (g_cat, leave, back_toep, fall_mat, skip, a_row, place),
        scalars=(6,),
    )
    shape = ((GROUPS * WIDTH, LENGTH), BF16)
    grad_first, grad_second, grad_third, grad_residue, grad_skip = call(
        finish_kernel,
        [shape, shape, shape, ((GROUPS, MODES), F32), ((1, GROUPS * WIDTH), F32)],
        [((ROWS, 128), BF16), ((ROWS, 256), F32)],
        (
            parts, conv, mixed, grad_out, first, second, rise_mat, fall_mat, start_decay, later_decay,
            from_later, from_earlier, a_row,
        ),
    )
    return grad_first, grad_second, grad_third, grad_residue, grad_skip.reshape(GROUPS * WIDTH)


def on_device(first, second, third, grad_heads, residue, decay_rate, skip_gain):
    grad_out = lax.all_to_all(
        grad_heads.reshape(SPANS, GROUPS * WIDTH, SPAN), "ch", split_axis=0, concat_axis=0, tiled=True
    )
    place = lax.axis_index("ctx").astype(jnp.int32).reshape(1)

    def exchange(payload):
        return lax.all_to_all(payload, "ctx", split_axis=0, concat_axis=0, tiled=True)

    return local(first, second, third, grad_out, exchange, residue, decay_rate, skip_gain, place)


def solution(mesh):
    return jax.shard_map(
        on_device,
        mesh=mesh,
        in_specs=(
            P("ch", "ctx"),
            P("ch", "ctx"),
            P("ch", "ctx"),
            P(None, ("ctx", "ch")),
            P("ch", None),
            P("ch", None),
            P("ch"),
        ),
        out_specs=(P("ch", "ctx"), P("ch", "ctx"), P("ch", "ctx"), P("ch", None), P("ch")),
        check_vma=False,
    )
```

```python
import jax
import jax.numpy as jnp
from jax import lax
from jax.experimental import pallas as pl
from jax.experimental.pallas import tpu as pltpu
from jax.sharding import PartitionSpec as P

F32, BF16 = jnp.float32, jnp.bfloat16
SPAN = 128
SPANS = 64
GROUPS, WIDTH, MODES = 2, 16, 16
ROWS = SPANS * WIDTH
LENGTH = SPAN * SPANS
CTX = 8
TOKENS = LENGTH * CTX


def iota(shape, dim):
    return lax.broadcasted_iota(jnp.int32, shape, dim)


def high(x):
    return x.astype(BF16)


def low(x):
    return (x - x.astype(BF16).astype(F32)).astype(BF16)


def dot(a, b):
    return jnp.dot(a, b, preferred_element_type=F32)


def halves(x):
    return x[:, :128] + x[:, 128:]


def state_matrix(a_row, age):
    decay = jnp.exp(-a_row * age)
    lane_group = (iota((128, 128), 1) % 32) // MODES
    out = []
    for g in range(GROUPS):
        mine = jnp.where(lane_group == g, decay, 0.0)
        block = jnp.concatenate([high(mine), low(mine)], axis=1)
        out += [block, block]
    return jnp.concatenate(out, axis=0)


def mode_matrix(a_col, w_col, age):
    wave = w_col * jnp.exp(-a_col * age)
    row = iota((128, 128), 0)
    part = jnp.where(row < 64, wave.astype(BF16).astype(F32), low(wave).astype(F32))
    row_group = (row % 32) // MODES
    return jnp.concatenate(
        [jnp.where(row_group == g, part, 0.0).astype(BF16) for g in range(GROUPS)], axis=1
    )


def quad_split(x, lane):
    top = x.astype(BF16).astype(F32)
    return jnp.where((lane // 32) % 2 == 0, top, x - top).astype(BF16)


def toeplitz(a_s, w_s, g, gap):
    near = jnp.maximum(gap, 0).astype(F32)
    total = jnp.zeros((SPAN, SPAN), F32)
    for r in range(MODES):
        total = total + w_s[g, r] * jnp.exp(-a_s[g, r] * near)
    total = jnp.where(gap >= 0, total, 0.0)
    block = jnp.concatenate([high(total), low(total)], axis=1)
    return jnp.concatenate([block, block], axis=0)


def begin(pairs, sems, first=0):
    copies = [
        pltpu.make_async_copy(source, target, sems.at[first + i]) for i, (source, target) in enumerate(pairs)
    ]
    for copy in copies:
        copy.start()
    return copies


def finish(copies):
    for copy in copies:
        copy.wait()


def forward_kernel(
    first_hbm, second_hbm, a_row, a_col, w_col, a_s, w_s, skip,
    x_cat_hbm, x_turn_hbm, conv_hbm, enter_hbm, back_toep_hbm, mats_hbm,
    first, second, x_cat, x_turn, conv, enter, back_toep, mats, states, toep, sems,
):
    inputs = begin([(first_hbm, first), (second_hbm, second)], sems)
    a = a_row[...]
    row = iota((128, 128), 0)
    col = iota((128, 128), 1)
    token = row.astype(F32)
    lane_token = col.astype(F32)
    mats[0] = mode_matrix(a_col[...], w_col[...], lane_token)
    mats[1] = mode_matrix(a_col[...], w_col[...], 127.0 - lane_token)
    for g in range(GROUPS):
        toep[g] = toeplitz(a_s, w_s, g, col - row)
        back_toep[g] = toeplitz(a_s, w_s, g, row - col)
    outputs = begin([(back_toep, back_toep_hbm), (mats, mats_hbm)], sems, 2)
    finish(inputs)
    for n in range(SPANS):
        at, here = pl.ds(n * WIDTH, WIDTH), pl.ds(n * SPAN, SPAN)
        x = first[:, here].astype(F32) * second[:, here].astype(F32)
        hi, lo = high(x), low(x)
        for g in range(GROUPS):
            c = slice(g * WIDTH, (g + 1) * WIDTH)
            x_cat[at, pl.ds(256 * g, 128)] = hi[c]
            x_cat[at, pl.ds(256 * g + 128, 128)] = lo[c]
    outputs += begin([(x_cat, x_cat_hbm)], sems, 4)
    states[...] = halves(dot(x_cat[...], state_matrix(a, 128.0 - token)))
    step = jnp.exp(-a * 128.0)
    carry = jnp.zeros((WIDTH, 128), F32)
    for n in range(SPANS):
        at = pl.ds(n * WIDTH, WIDTH)
        enter[at, :] = carry
        carry = carry * step + states[at, :]
    enter[pl.ds(ROWS, WIDTH), :] = carry
    enter[pl.ds(ROWS + WIDTH, 8), :] = jnp.broadcast_to(a, (8, 128))
    outputs += begin([(enter, enter_hbm)], sems, 5)
    lane = iota((ROWS, 128), 1)
    conv[...] = dot(quad_split(enter[pl.ds(0, ROWS), :], lane), mats[0])
    for g in range(GROUPS):
        mine = pl.ds(256 * g, 256)
        here = pl.ds(128 * g, 128)
        x = x_cat[:, mine]
        gain = jnp.concatenate([skip[g]] * SPANS, axis=0)
        gated = x[:, :128].astype(F32) + x[:, 128:].astype(F32)
        conv[:, here] = conv[:, here] + halves(dot(x, toep[g])) + gain * gated
        x_turn[g] = x.T
    outputs += begin([(x_turn, x_turn_hbm), (conv, conv_hbm)], sems, 6)
    finish(outputs)


def middle_kernel(
    grad_out, third_hbm, x_cat_hbm, x_turn_hbm, enter_hbm,
    payload_hbm, grad_out_hbm,
    third, x_cat, x_turn, enter, g_cat, states, payload, sems,
):
    early = begin([(third_hbm, third)], sems)
    enter_in, turn_in, cat_in = begin(
        [(enter_hbm, enter), (x_turn_hbm, x_turn), (x_cat_hbm, x_cat)], sems, 1
    )
    outputs = begin([(grad_out, grad_out_hbm)], sems, 4)
    row = iota((128, 128), 0)
    col = iota((128, 128), 1)
    token = row.astype(F32)
    finish(early)
    for n in range(SPANS):
        at, here = pl.ds(n * WIDTH, WIDTH), pl.ds(n * SPAN, SPAN)
        y = grad_out[n].astype(F32) * third[:, here].astype(F32)
        hi, lo = high(y), low(y)
        for g in range(GROUPS):
            c = slice(g * WIDTH, (g + 1) * WIDTH)
            g_cat[at, pl.ds(256 * g, 128)] = hi[c]
            g_cat[at, pl.ds(256 * g + 128, 128)] = lo[c]
    finish([enter_in])
    a = enter[pl.ds(ROWS + WIDTH, 1), :]
    states[...] = halves(dot(g_cat[...], state_matrix(a, token + 1.0)))
    finish([turn_in])
    cross = []
    for g in range(GROUPS):
        four = dot(x_turn[g], g_cat[:, pl.ds(256 * g, 256)])
        four = halves(four[:128] + four[128:])
        four = jnp.where(col >= row, four, 0.0)
        cross += [high(four), low(four)]
    near = halves(dot(jnp.concatenate(cross, axis=1), state_matrix(a, token - 64.0)))
    near = near * jnp.exp(a * (token - 64.0))
    near = jnp.sum(near.reshape(16, 8, 128), axis=0)
    step = jnp.exp(-a * 128.0)
    carry = jnp.zeros((WIDTH, 128), F32)
    far = jnp.zeros((WIDTH, 128), F32)
    for n in reversed(range(SPANS)):
        at = pl.ds(n * WIDTH, WIDTH)
        now = states[at, :]
        far = far + now * enter[at, :]
        carry = carry * step + now
    weight = near + (far[:8] + far[8:]) * jnp.exp(a)
    finish([cat_in])
    total = []
    for g in range(GROUPS):
        mine = jnp.zeros((WIDTH, SPAN), F32)
        hi, lo = pl.ds(256 * g, 128), pl.ds(256 * g + 128, 128)
        for n in range(SPANS):
            at = pl.ds(n * WIDTH, WIDTH)
            x = x_cat[at, hi].astype(F32) + x_cat[at, lo].astype(F32)
            y = g_cat[at, hi].astype(F32) + g_cat[at, lo].astype(F32)
            mine = mine + x * y
        total.append(mine)
    direct = lax.dot_general(
        jnp.ones((8, SPAN), F32),
        jnp.concatenate(total * 4, axis=0),
        (((1,), (1,)), ((), ())),
        precision=lax.Precision.HIGHEST,
        preferred_element_type=F32,
    )
    quarter = iota((8, 128), 1) // 32
    back = jnp.where(
        quarter == 0, carry[:8], jnp.where(quarter == 1, carry[8:], jnp.where(quarter == 2, weight, direct))
    )
    state = enter[pl.ds(ROWS, WIDTH), :]
    ahead = jnp.where(quarter == 0, state[:8, :], state[8:, :])
    for k in range(CTX):
        payload[k, :8, :] = back
        payload[k, 8:, :] = ahead
    finish(outputs + begin([(payload, payload_hbm)], sems, 5))


def backward_kernel(
    grad_out_hbm, third_hbm, back_toep_hbm, mats_hbm, a_row, skip, place, payload_hbm,
    mixed_hbm, small_hbm,
    grad_out, third, back_toep, mats, g_cat, states, leave, mixed, small, sems,
):
    early = begin(
        [(grad_out_hbm, grad_out), (third_hbm, third), (back_toep_hbm, back_toep), (mats_hbm, mats)], sems
    )
    a = a_row[...]
    token = iota((128, 128), 0).astype(F32)
    wide = jnp.broadcast_to(a, (8, 128)) * float(LENGTH)
    is_state = iota((8, 128), 1) < 64
    me = place[0]
    for k in range(CTX):
        after = jnp.maximum(k - me - 1, 0).astype(F32)
        before = jnp.maximum(me - 1 - k, 0).astype(F32)
        later = jnp.where(k > me, 1.0, 0.0)
        earlier = jnp.where(k < me, 1.0, 0.0)
        small[k] = jnp.where(is_state, jnp.exp(-wide * after) * later, 1.0)
        small[CTX + k] = jnp.exp(-wide * before) * earlier
    small[2 * CTX] = jnp.broadcast_to(a, (8, 128))
    outputs = begin([(small, small_hbm)], sems, 4)
    finish(early)
    for n in range(SPANS):
        at, here = pl.ds(n * WIDTH, WIDTH), pl.ds(n * SPAN, SPAN)
        y = grad_out[n].astype(F32) * third[:, here].astype(F32)
        hi, lo = high(y), low(y)
        for g in range(GROUPS):
            c = slice(g * WIDTH, (g + 1) * WIDTH)
            g_cat[at, pl.ds(256 * g, 128)] = hi[c]
            g_cat[at, pl.ds(256 * g + 128, 128)] = lo[c]
    states[...] = halves(dot(g_cat[...], state_matrix(a, token + 1.0)))
    step = jnp.exp(-a * 128.0)
    carry = jnp.zeros((WIDTH, 128), F32)
    for n in reversed(range(SPANS)):
        at = pl.ds(n * WIDTH, WIDTH)
        leave[at, :] = carry
        carry = carry * step + states[at, :]
    lane = iota((ROWS, 128), 1)
    mixed[...] = dot(quad_split(leave[...], lane), mats[1])
    for g in range(GROUPS):
        here = pl.ds(128 * g, 128)
        y = g_cat[:, pl.ds(256 * g, 256)]
        gain = jnp.concatenate([skip[g]] * SPANS, axis=0)
        grad_conv = y[:, :128].astype(F32) + y[:, 128:].astype(F32)
        mixed[:, here] = mixed[:, here] + halves(dot(y, back_toep[g])) + gain * grad_conv
    outputs += begin([(mixed, mixed_hbm)], sems, 5)
    finish(outputs)


CHUNKS = 4
CHUNK_SPANS = SPANS // CHUNKS
CHUNK_ROWS = ROWS // CHUNKS
CHUNK_TOKENS = LENGTH // CHUNKS


def finish_kernel(
    parts, small_hbm, mats_hbm, conv_hbm, mixed_hbm, grad_out_hbm, first_hbm, second_hbm,
    grad_first_hbm, grad_second_hbm, grad_third_hbm, grad_residue_hbm, grad_skip_hbm,
    small, mats, conv, mixed, grad_out, first, second, grad_first, grad_second, grad_third, grad_residue, grad_skip, decays,
    sems,
):
    def rows_of(c):
        return pl.ds(c * CHUNK_ROWS, CHUNK_ROWS)

    def spans_of(c):
        return pl.ds(c * CHUNK_SPANS, CHUNK_SPANS)

    def tokens_of(c):
        return pl.ds(c * CHUNK_TOKENS, CHUNK_TOKENS)

    early = begin([(small_hbm, small), (mats_hbm, mats)], sems)
    used = 2
    third_in, gate_in = [], []
    for c in range(CHUNKS):
        third_in.append(
            begin(
                [
                    (conv_hbm.at[rows_of(c), :], conv.at[rows_of(c), :]),
                    (grad_out_hbm.at[spans_of(c)], grad_out.at[spans_of(c)]),
                ],
                sems,
                used,
            )
        )
        used += 2
    for c in range(CHUNKS):
        gate_in.append(
            begin(
                [
                    (mixed_hbm.at[rows_of(c), :], mixed.at[rows_of(c), :]),
                    (first_hbm.at[:, tokens_of(c)], first.at[:, tokens_of(c)]),
                    (second_hbm.at[:, tokens_of(c)], second.at[:, tokens_of(c)]),
                ],
                sems,
                used,
            )
        )
        used += 3
    finish(early)
    a = small[2 * CTX, 0:1, :]
    quarter = iota((8, 128), 1) // 32
    back = jnp.zeros((8, 128), F32)
    ahead = jnp.zeros((8, 128), F32)
    running = jnp.zeros((8, 128), F32)
    far = jnp.zeros((8, 128), F32)
    block_step = jnp.exp(-a * float(LENGTH))
    for k in range(CTX):
        later, earlier = parts[k, :8, :], parts[k, 8:, :]
        back = back + later * small[k]
        ahead = ahead + earlier * small[CTX + k]
        far = far + later * running
        running = running * block_step + earlier

    def spread(x, q):
        x = jnp.where(quarter == q, x, 0.0)
        x = x + pltpu.roll(x, 32, 1)
        return x + pltpu.roll(x, 64, 1)

    def rows(x):
        return jnp.concatenate([spread(x, 0), spread(x, 1)], axis=0)

    span = iota((SPANS, 128), 0).astype(F32)
    decays[0] = jnp.exp(-a * (128.0 * span))
    decays[1] = jnp.exp(-a * (128.0 * (SPANS - 1.0 - span)))
    lane = iota((CHUNK_ROWS, 128), 1)

    def fix(x, side, c):
        decay = decays[side, spans_of(c), :].reshape(CHUNK_SPANS, 1, 128)
        whole = (decay * x.reshape(1, WIDTH, 128)).reshape(CHUNK_ROWS, 128)
        return dot(quad_split(whole, lane), mats[side])

    def channels(x, i):
        x = x[i * WIDTH : (i + 1) * WIDTH]
        return jnp.concatenate([x[:, :128], x[:, 128:]], axis=0)

    outputs = []
    entering, leaving = rows(ahead), rows(back)
    for c in range(CHUNKS):
        add = fix(entering, 0, c)
        finish(third_in[c])
        full = conv[rows_of(c), :] + add
        for i in range(CHUNK_SPANS):
            n = c * CHUNK_SPANS + i
            grad_third[:, pl.ds(n * SPAN, SPAN)] = (grad_out[n].astype(F32) * channels(full, i)).astype(BF16)
        outputs += begin([(grad_third.at[:, tokens_of(c)], grad_third_hbm.at[:, tokens_of(c)])], sems, used)
        used += 1
    near = spread(back, 2)
    crossed = (spread(far, 0) + spread(far, 1)) * jnp.exp(a)
    weight = jnp.sum(near + crossed, axis=0, keepdims=True)
    weight = weight * jnp.sqrt(2.0 * a) * (1.0 / (float(WIDTH * TOKENS) ** 0.5))
    grad_residue[0:1, :] = weight[:, :MODES]
    grad_residue[1:2, :] = pltpu.roll(weight, 128 - MODES, 1)[:, :MODES]
    direct = pltpu.roll(back, 32, 1)[0:1] * (1.0 / (float(TOKENS) ** 0.5))
    grad_skip[...] = direct[:, : GROUPS * WIDTH]
    outputs += begin([(grad_residue, grad_residue_hbm), (grad_skip, grad_skip_hbm)], sems, used)
    used += 2
    for c in range(CHUNKS):
        add = fix(leaving, 1, c)
        finish(gate_in[c])
        full = mixed[rows_of(c), :] + add
        for i in range(CHUNK_SPANS):
            here = pl.ds((c * CHUNK_SPANS + i) * SPAN, SPAN)
            part = channels(full, i)
            grad_first[:, here] = (part * second[:, here].astype(F32)).astype(BF16)
            grad_second[:, here] = (part * first[:, here].astype(F32)).astype(BF16)
        outputs += begin(
            [
                (grad_first.at[:, tokens_of(c)], grad_first_hbm.at[:, tokens_of(c)]),
                (grad_second.at[:, tokens_of(c)], grad_second_hbm.at[:, tokens_of(c)]),
            ],
            sems,
            used,
        )
        used += 2
    finish(outputs)


FINISH_COPIES = 2 + 5 * CHUNKS + 3 * CHUNKS + 2


def call(kernel, outs, scratch, copies, args, vmem=(), smem=()):
    def space(i):
        return pltpu.VMEM if i in vmem else pltpu.SMEM if i in smem else pltpu.HBM

    return pl.pallas_call(
        kernel,
        out_shape=tuple(pltpu.HBM(s, d) for s, d in outs),
        in_specs=[pl.BlockSpec(memory_space=space(i)) for i in range(len(args))],
        out_specs=tuple(pl.BlockSpec(memory_space=pltpu.HBM) for _ in outs),
        scratch_shapes=[pltpu.VMEM(s, d) for s, d in scratch] + [pltpu.SemaphoreType.DMA((copies,))],
        compiler_params=pltpu.CompilerParams(vmem_limit_bytes=40 << 20),
    )(
        *(
            pltpu.with_memory_space_constraint(x, pltpu.HBM) if space(i) == pltpu.HBM else x
            for i, x in enumerate(args)
        )
    )


def prepare(residue, decay_rate, skip_gain):
    weight = residue * jnp.sqrt(2.0 * decay_rate)
    a_row = jnp.tile(decay_rate.reshape(1, 32), (1, 4))
    a_col = jnp.tile(decay_rate.reshape(32, 1), (4, 1))
    w_col = jnp.tile(weight.reshape(32, 1), (4, 1))
    return a_row, a_col, w_col, weight, skip_gain.reshape(GROUPS, WIDTH, 1)


GATE = ((GROUPS * WIDTH, LENGTH), BF16)
ARRIVED = ((SPANS, GROUPS * WIDTH, SPAN), BF16)
CAT = ((ROWS, 512), BF16)
TURN = ((GROUPS, 256, ROWS), BF16)
WHOLE = ((ROWS, 256), F32)
STATES = ((ROWS, 128), F32)
ENTER = ((ROWS + WIDTH + 8, 128), F32)
TOEP = ((GROUPS, 256, 256), BF16)
MATS = ((2, 128, 256), BF16)
PARTS = ((CTX, 16, 128), F32)
SMALL = ((2 * CTX + 1, 8, 128), F32)
RESIDUE = ((GROUPS, MODES), F32)
SKIP = ((1, GROUPS * WIDTH), F32)


def local(first, second, third, grad_out, exchange, residue, decay_rate, skip_gain, place):
    a_row, a_col, w_col, weight, skip = prepare(residue, decay_rate, skip_gain)
    outs = [CAT, TURN, WHOLE, ENTER, TOEP, MATS]
    x_cat, x_turn, conv, enter, back_toep, mats = call(
        forward_kernel,
        outs,
        [GATE, GATE] + outs + [STATES, TOEP],
        8,
        (first, second, a_row, a_col, w_col, decay_rate, weight, skip),
        vmem=(2, 3, 4, 7),
        smem=(5, 6),
    )
    payload, grad_out = call(
        middle_kernel,
        [PARTS, ARRIVED],
        [GATE, CAT, TURN, ENTER, CAT, STATES, PARTS],
        6,
        (grad_out, third, x_cat, x_turn, enter),
        vmem=(0,),
    )
    parts = exchange(payload)
    mixed, small = call(
        backward_kernel,
        [WHOLE, SMALL],
        [ARRIVED, GATE, TOEP, MATS, CAT, STATES, STATES, WHOLE, SMALL],
        6,
        (grad_out, third, back_toep, mats, a_row, skip, place, payload),
        vmem=(4, 5),
        smem=(6,),
    )
    outs = [GATE, GATE, GATE, RESIDUE, SKIP]
    grad_first, grad_second, grad_third, grad_residue, grad_skip = call(
        finish_kernel,
        outs,
        [SMALL, MATS, WHOLE, WHOLE, ARRIVED, GATE, GATE] + outs + [((2, SPANS, 128), F32)],
        FINISH_COPIES,
        (parts, small, mats, conv, mixed, grad_out, first, second),
        vmem=(0,),
    )
    return grad_first, grad_second, grad_third, grad_residue, grad_skip.reshape(GROUPS * WIDTH)


def on_device(first, second, third, grad_heads, residue, decay_rate, skip_gain):
    grad_out = lax.all_to_all(
        grad_heads.reshape(SPANS, GROUPS * WIDTH, SPAN), "ch", split_axis=0, concat_axis=0, tiled=True
    )
    place = lax.axis_index("ctx").astype(jnp.int32).reshape(1)

    def exchange(payload):
        return lax.all_to_all(payload, "ctx", split_axis=0, concat_axis=0, tiled=True)

    return local(first, second, third, grad_out, exchange, residue, decay_rate, skip_gain, place)


def solution(mesh):
    return jax.shard_map(
        on_device,
        mesh=mesh,
        in_specs=(
            P("ch", "ctx"),
            P("ch", "ctx"),
            P("ch", "ctx"),
            P(None, ("ctx", "ch")),
            P("ch", None),
            P("ch", None),
            P("ch"),
        ),
        out_specs=(P("ch", "ctx"), P("ch", "ctx"), P("ch", "ctx"), P("ch", None), P("ch")),
        check_vma=False,
    )
```

```python
import jax
import jax.numpy as jnp
from jax import lax
from jax.experimental import pallas as pl
from jax.experimental.pallas import tpu as pltpu
from jax.sharding import PartitionSpec as P

F32, BF16 = jnp.float32, jnp.bfloat16
SPAN = 128
SPANS = 64
GROUPS, WIDTH, MODES = 2, 16, 16
ROWS = SPANS * WIDTH
LENGTH = SPAN * SPANS
CTX = 8
TOKENS = LENGTH * CTX


def iota(shape, dim):
    return lax.broadcasted_iota(jnp.int32, shape, dim)


def high(x):
    return x.astype(BF16)


def low(x):
    return (x - x.astype(BF16).astype(F32)).astype(BF16)


def dot(a, b):
    return jnp.dot(a, b, preferred_element_type=F32)


def halves(x):
    return x[:, :128] + x[:, 128:]


def state_matrix(a_row, age):
    decay = jnp.exp(-a_row * age)
    lane_group = (iota((128, 128), 1) % 32) // MODES
    out = []
    for g in range(GROUPS):
        mine = jnp.where(lane_group == g, decay, 0.0)
        block = jnp.concatenate([high(mine), low(mine)], axis=1)
        out += [block, block]
    return jnp.concatenate(out, axis=0)


def mode_matrix(a_col, w_col, age):
    wave = w_col * jnp.exp(-a_col * age)
    row = iota((128, 128), 0)
    part = jnp.where(row < 64, wave.astype(BF16).astype(F32), low(wave).astype(F32))
    row_group = (row % 32) // MODES
    return jnp.concatenate(
        [jnp.where(row_group == g, part, 0.0).astype(BF16) for g in range(GROUPS)], axis=1
    )


def quad_split(x, lane):
    top = x.astype(BF16).astype(F32)
    return jnp.where((lane // 32) % 2 == 0, top, x - top).astype(BF16)


def toeplitz(a_s, w_s, g, gap):
    near = jnp.maximum(gap, 0).astype(F32)
    total = jnp.zeros((SPAN, SPAN), F32)
    for r in range(MODES):
        total = total + w_s[g, r] * jnp.exp(-a_s[g, r] * near)
    total = jnp.where(gap >= 0, total, 0.0)
    block = jnp.concatenate([high(total), low(total)], axis=1)
    return jnp.concatenate([block, block], axis=0)


def begin(pairs, sems, first=0):
    copies = [
        pltpu.make_async_copy(source, target, sems.at[first + i]) for i, (source, target) in enumerate(pairs)
    ]
    for copy in copies:
        copy.start()
    return copies


def finish(copies):
    for copy in copies:
        copy.wait()


def forward_kernel(
    first_hbm, second_hbm, a_row, a_col, w_col, a_s, w_s, skip,
    x_cat_hbm, x_turn_hbm, conv_hbm, enter_hbm, back_toep_hbm, mats_hbm,
    first, second, x_cat, x_turn, conv, enter, back_toep, mats, states, toep, sems,
):
    inputs = begin([(first_hbm, first), (second_hbm, second)], sems)
    a = a_row[...]
    row = iota((128, 128), 0)
    col = iota((128, 128), 1)
    token = row.astype(F32)
    lane_token = col.astype(F32)
    mats[0] = mode_matrix(a_col[...], w_col[...], lane_token)
    mats[1] = mode_matrix(a_col[...], w_col[...], 127.0 - lane_token)
    for g in range(GROUPS):
        toep[g] = toeplitz(a_s, w_s, g, col - row)
        back_toep[g] = toeplitz(a_s, w_s, g, row - col)
    outputs = begin([(back_toep, back_toep_hbm), (mats, mats_hbm)], sems, 2)
    finish(inputs)
    for n in range(SPANS):
        at, here = pl.ds(n * WIDTH, WIDTH), pl.ds(n * SPAN, SPAN)
        x = first[:, here].astype(F32) * second[:, here].astype(F32)
        hi, lo = high(x), low(x)
        for g in range(GROUPS):
            c = slice(g * WIDTH, (g + 1) * WIDTH)
            x_cat[at, pl.ds(256 * g, 128)] = hi[c]
            x_cat[at, pl.ds(256 * g + 128, 128)] = lo[c]
    outputs += begin([(x_cat, x_cat_hbm)], sems, 4)
    states[...] = halves(dot(x_cat[...], state_matrix(a, 128.0 - token)))
    step = jnp.exp(-a * 128.0)
    carry = jnp.zeros((WIDTH, 128), F32)
    for n in range(SPANS):
        at = pl.ds(n * WIDTH, WIDTH)
        enter[at, :] = carry
        carry = carry * step + states[at, :]
    enter[pl.ds(ROWS, WIDTH), :] = carry
    enter[pl.ds(ROWS + WIDTH, 8), :] = jnp.broadcast_to(a, (8, 128))
    outputs += begin([(enter, enter_hbm)], sems, 5)
    lane = iota((ROWS, 128), 1)
    conv[...] = dot(quad_split(enter[pl.ds(0, ROWS), :], lane), mats[0])
    for g in range(GROUPS):
        mine = pl.ds(256 * g, 256)
        here = pl.ds(128 * g, 128)
        x = x_cat[:, mine]
        gain = jnp.concatenate([skip[g]] * SPANS, axis=0)
        gated = x[:, :128].astype(F32) + x[:, 128:].astype(F32)
        conv[:, here] = conv[:, here] + halves(dot(x, toep[g])) + gain * gated
        x_turn[g] = x.T
    outputs += begin([(x_turn, x_turn_hbm), (conv, conv_hbm)], sems, 6)
    finish(outputs)


FIRST = 36
CH_ORDER = [FIRST if p == 0 else 0 if p == FIRST else p for p in range(SPANS)]
CTX_ORDER = [5, 1, 3, 7, 2, 0, 4, 6]
CTX_PLACE = [CTX_ORDER.index(k) for k in range(CTX)]
RUNS = [(0, 1)] + [(i, min(i + 5, FIRST)) for i in range(1, FIRST, 5)] + [(FIRST, FIRST + 1)]
RUNS += [(i, min(i + 5, SPANS)) for i in range(FIRST + 1, SPANS, 5)]


def swap_copies(source, target, sems, first=0):
    return begin(
        [
            (source.at[pl.ds(CH_ORDER[i], j - i)], target.at[pl.ds(i, j - i)])
            for i, j in RUNS
        ],
        sems,
        first,
    )


def swap_kernel(heads, swapped, sems):
    finish(swap_copies(heads, swapped, sems))


def swap(heads):
    return pl.pallas_call(
        swap_kernel,
        out_shape=jax.ShapeDtypeStruct(heads.shape, heads.dtype),
        in_specs=[pl.BlockSpec(memory_space=pltpu.HBM)],
        out_specs=pl.BlockSpec(memory_space=pltpu.VMEM),
        scratch_shapes=[pltpu.SemaphoreType.DMA((len(RUNS),))],
    )(pltpu.with_memory_space_constraint(heads, pltpu.HBM))


def middle_kernel(
    grad_out, third_hbm, x_cat_hbm, x_turn_hbm, enter_hbm,
    payload_hbm, grad_out_hbm,
    third, x_cat, x_turn, enter, g_cat, states, payload, sems,
):
    early = begin([(third_hbm, third)], sems)
    enter_in, turn_in, cat_in = begin(
        [(enter_hbm, enter), (x_turn_hbm, x_turn), (x_cat_hbm, x_cat)], sems, 1
    )
    outputs = swap_copies(grad_out, grad_out_hbm, sems, 5)
    row = iota((128, 128), 0)
    col = iota((128, 128), 1)
    token = row.astype(F32)
    finish(early)
    for n in range(SPANS):
        at, here = pl.ds(n * WIDTH, WIDTH), pl.ds(n * SPAN, SPAN)
        y = grad_out[CH_ORDER[n]].astype(F32) * third[:, here].astype(F32)
        hi, lo = high(y), low(y)
        for g in range(GROUPS):
            c = slice(g * WIDTH, (g + 1) * WIDTH)
            g_cat[at, pl.ds(256 * g, 128)] = hi[c]
            g_cat[at, pl.ds(256 * g + 128, 128)] = lo[c]
    finish([enter_in])
    a = enter[pl.ds(ROWS + WIDTH, 1), :]
    states[...] = halves(dot(g_cat[...], state_matrix(a, token + 1.0)))
    finish([turn_in])
    cross = []
    for g in range(GROUPS):
        four = dot(x_turn[g], g_cat[:, pl.ds(256 * g, 256)])
        four = halves(four[:128] + four[128:])
        four = jnp.where(col >= row, four, 0.0)
        cross += [high(four), low(four)]
    near = halves(dot(jnp.concatenate(cross, axis=1), state_matrix(a, token - 64.0)))
    near = near * jnp.exp(a * (token - 64.0))
    near = jnp.sum(near.reshape(16, 8, 128), axis=0)
    step = jnp.exp(-a * 128.0)
    carry = jnp.zeros((WIDTH, 128), F32)
    far = jnp.zeros((WIDTH, 128), F32)
    for n in reversed(range(SPANS)):
        at = pl.ds(n * WIDTH, WIDTH)
        now = states[at, :]
        far = far + now * enter[at, :]
        carry = carry * step + now
    weight = near + (far[:8] + far[8:]) * jnp.exp(a)
    finish([cat_in])
    total = []
    for g in range(GROUPS):
        mine = jnp.zeros((WIDTH, SPAN), F32)
        hi, lo = pl.ds(256 * g, 128), pl.ds(256 * g + 128, 128)
        for n in range(SPANS):
            at = pl.ds(n * WIDTH, WIDTH)
            x = x_cat[at, hi].astype(F32) + x_cat[at, lo].astype(F32)
            y = g_cat[at, hi].astype(F32) + g_cat[at, lo].astype(F32)
            mine = mine + x * y
        total.append(mine)
    direct = lax.dot_general(
        jnp.ones((8, SPAN), F32),
        jnp.concatenate(total * 4, axis=0),
        (((1,), (1,)), ((), ())),
        precision=lax.Precision.HIGHEST,
        preferred_element_type=F32,
    )
    quarter = iota((8, 128), 1) // 32
    back = jnp.where(
        quarter == 0, carry[:8], jnp.where(quarter == 1, carry[8:], jnp.where(quarter == 2, weight, direct))
    )
    state = enter[pl.ds(ROWS, WIDTH), :]
    ahead = jnp.where(quarter == 0, state[:8, :], state[8:, :])
    for k in range(CTX):
        payload[k, :8, :] = back
        payload[k, 8:, :] = ahead
    finish(outputs + begin([(payload, payload_hbm)], sems, 4))


def backward_kernel(
    grad_out_hbm, third_hbm, back_toep_hbm, mats_hbm, a_row, skip, place, payload_hbm,
    mixed_hbm, small_hbm,
    grad_out, third, back_toep, mats, g_cat, states, leave, mixed, small, sems,
):
    early = begin(
        [(grad_out_hbm, grad_out), (third_hbm, third), (back_toep_hbm, back_toep), (mats_hbm, mats)], sems
    )
    a = a_row[...]
    token = iota((128, 128), 0).astype(F32)
    wide = jnp.broadcast_to(a, (8, 128)) * float(LENGTH)
    is_state = iota((8, 128), 1) < 64
    me = place[0]
    for k in range(CTX):
        after = jnp.maximum(k - me - 1, 0).astype(F32)
        before = jnp.maximum(me - 1 - k, 0).astype(F32)
        later = jnp.where(k > me, 1.0, 0.0)
        earlier = jnp.where(k < me, 1.0, 0.0)
        small[k] = jnp.where(is_state, jnp.exp(-wide * after) * later, 1.0)
        small[CTX + k] = jnp.exp(-wide * before) * earlier
    small[2 * CTX] = jnp.broadcast_to(a, (8, 128))
    outputs = begin([(small, small_hbm)], sems, 4)
    finish(early)
    for n in range(SPANS):
        at, here = pl.ds(n * WIDTH, WIDTH), pl.ds(n * SPAN, SPAN)
        y = grad_out[n].astype(F32) * third[:, here].astype(F32)
        hi, lo = high(y), low(y)
        for g in range(GROUPS):
            c = slice(g * WIDTH, (g + 1) * WIDTH)
            g_cat[at, pl.ds(256 * g, 128)] = hi[c]
            g_cat[at, pl.ds(256 * g + 128, 128)] = lo[c]
    states[...] = halves(dot(g_cat[...], state_matrix(a, token + 1.0)))
    step = jnp.exp(-a * 128.0)
    carry = jnp.zeros((WIDTH, 128), F32)
    for n in reversed(range(SPANS)):
        at = pl.ds(n * WIDTH, WIDTH)
        leave[at, :] = carry
        carry = carry * step + states[at, :]
    lane = iota((ROWS, 128), 1)
    mixed[...] = dot(quad_split(leave[...], lane), mats[1])
    for g in range(GROUPS):
        here = pl.ds(128 * g, 128)
        y = g_cat[:, pl.ds(256 * g, 256)]
        gain = jnp.concatenate([skip[g]] * SPANS, axis=0)
        grad_conv = y[:, :128].astype(F32) + y[:, 128:].astype(F32)
        mixed[:, here] = mixed[:, here] + halves(dot(y, back_toep[g])) + gain * grad_conv
    outputs += begin([(mixed, mixed_hbm)], sems, 5)
    finish(outputs)


CHUNKS = 4
CHUNK_SPANS = SPANS // CHUNKS
CHUNK_ROWS = ROWS // CHUNKS
CHUNK_TOKENS = LENGTH // CHUNKS


def finish_kernel(
    parts, small_hbm, mats_hbm, conv_hbm, mixed_hbm, grad_out_hbm, first_hbm, second_hbm,
    grad_first_hbm, grad_second_hbm, grad_third_hbm, grad_residue_hbm, grad_skip_hbm,
    small, mats, conv, mixed, grad_out, first, second, grad_first, grad_second, grad_third, grad_residue, grad_skip, decays,
    sems,
):
    def rows_of(c):
        return pl.ds(c * CHUNK_ROWS, CHUNK_ROWS)

    def spans_of(c):
        return pl.ds(c * CHUNK_SPANS, CHUNK_SPANS)

    def tokens_of(c):
        return pl.ds(c * CHUNK_TOKENS, CHUNK_TOKENS)

    early = begin([(small_hbm, small), (mats_hbm, mats)], sems)
    used = 2
    third_in, gate_in = [], []
    for c in range(CHUNKS):
        third_in.append(
            begin(
                [
                    (conv_hbm.at[rows_of(c), :], conv.at[rows_of(c), :]),
                    (grad_out_hbm.at[spans_of(c)], grad_out.at[spans_of(c)]),
                ],
                sems,
                used,
            )
        )
        used += 2
    for c in range(CHUNKS):
        gate_in.append(
            begin(
                [
                    (mixed_hbm.at[rows_of(c), :], mixed.at[rows_of(c), :]),
                    (first_hbm.at[:, tokens_of(c)], first.at[:, tokens_of(c)]),
                    (second_hbm.at[:, tokens_of(c)], second.at[:, tokens_of(c)]),
                ],
                sems,
                used,
            )
        )
        used += 3
    finish(early)
    a = small[2 * CTX, 0:1, :]
    quarter = iota((8, 128), 1) // 32
    back = jnp.zeros((8, 128), F32)
    ahead = jnp.zeros((8, 128), F32)
    running = jnp.zeros((8, 128), F32)
    far = jnp.zeros((8, 128), F32)
    block_step = jnp.exp(-a * float(LENGTH))
    for k in range(CTX):
        at = CTX_PLACE[k]
        later, earlier = parts[at, :8, :], parts[at, 8:, :]
        back = back + later * small[k]
        ahead = ahead + earlier * small[CTX + k]
        far = far + later * running
        running = running * block_step + earlier

    def spread(x, q):
        x = jnp.where(quarter == q, x, 0.0)
        x = x + pltpu.roll(x, 32, 1)
        return x + pltpu.roll(x, 64, 1)

    def rows(x):
        return jnp.concatenate([spread(x, 0), spread(x, 1)], axis=0)

    span = iota((SPANS, 128), 0).astype(F32)
    decays[0] = jnp.exp(-a * (128.0 * span))
    decays[1] = jnp.exp(-a * (128.0 * (SPANS - 1.0 - span)))
    lane = iota((CHUNK_ROWS, 128), 1)

    def fix(x, side, c):
        decay = decays[side, spans_of(c), :].reshape(CHUNK_SPANS, 1, 128)
        whole = (decay * x.reshape(1, WIDTH, 128)).reshape(CHUNK_ROWS, 128)
        return dot(quad_split(whole, lane), mats[side])

    def channels(x, i):
        x = x[i * WIDTH : (i + 1) * WIDTH]
        return jnp.concatenate([x[:, :128], x[:, 128:]], axis=0)

    outputs = []
    entering, leaving = rows(ahead), rows(back)
    for c in range(CHUNKS):
        add = fix(entering, 0, c)
        finish(third_in[c])
        full = conv[rows_of(c), :] + add
        for i in range(CHUNK_SPANS):
            n = c * CHUNK_SPANS + i
            grad_third[:, pl.ds(n * SPAN, SPAN)] = (grad_out[n].astype(F32) * channels(full, i)).astype(BF16)
        outputs += begin([(grad_third.at[:, tokens_of(c)], grad_third_hbm.at[:, tokens_of(c)])], sems, used)
        used += 1
    near = spread(back, 2)
    crossed = (spread(far, 0) + spread(far, 1)) * jnp.exp(a)
    weight = jnp.sum(near + crossed, axis=0, keepdims=True)
    weight = weight * jnp.sqrt(2.0 * a) * (1.0 / (float(WIDTH * TOKENS) ** 0.5))
    grad_residue[0:1, :] = weight[:, :MODES]
    grad_residue[1:2, :] = pltpu.roll(weight, 128 - MODES, 1)[:, :MODES]
    direct = pltpu.roll(back, 32, 1)[0:1] * (1.0 / (float(TOKENS) ** 0.5))
    grad_skip[...] = direct[:, : GROUPS * WIDTH]
    outputs += begin([(grad_residue, grad_residue_hbm), (grad_skip, grad_skip_hbm)], sems, used)
    used += 2
    for c in range(CHUNKS):
        add = fix(leaving, 1, c)
        finish(gate_in[c])
        full = mixed[rows_of(c), :] + add
        for i in range(CHUNK_SPANS):
            here = pl.ds((c * CHUNK_SPANS + i) * SPAN, SPAN)
            part = channels(full, i)
            grad_first[:, here] = (part * second[:, here].astype(F32)).astype(BF16)
            grad_second[:, here] = (part * first[:, here].astype(F32)).astype(BF16)
        outputs += begin(
            [
                (grad_first.at[:, tokens_of(c)], grad_first_hbm.at[:, tokens_of(c)]),
                (grad_second.at[:, tokens_of(c)], grad_second_hbm.at[:, tokens_of(c)]),
            ],
            sems,
            used,
        )
        used += 2
    finish(outputs)


FINISH_COPIES = 2 + 5 * CHUNKS + 3 * CHUNKS + 2


def call(kernel, outs, scratch, copies, args, vmem=(), smem=()):
    def space(i):
        return pltpu.VMEM if i in vmem else pltpu.SMEM if i in smem else pltpu.HBM

    return pl.pallas_call(
        kernel,
        out_shape=tuple(pltpu.HBM(s, d) for s, d in outs),
        in_specs=[pl.BlockSpec(memory_space=space(i)) for i in range(len(args))],
        out_specs=tuple(pl.BlockSpec(memory_space=pltpu.HBM) for _ in outs),
        scratch_shapes=[pltpu.VMEM(s, d) for s, d in scratch] + [pltpu.SemaphoreType.DMA((copies,))],
        compiler_params=pltpu.CompilerParams(vmem_limit_bytes=40 << 20),
    )(
        *(
            pltpu.with_memory_space_constraint(x, pltpu.HBM) if space(i) == pltpu.HBM else x
            for i, x in enumerate(args)
        )
    )


def prepare(residue, decay_rate, skip_gain):
    weight = residue * jnp.sqrt(2.0 * decay_rate)
    a_row = jnp.tile(decay_rate.reshape(1, 32), (1, 4))
    a_col = jnp.tile(decay_rate.reshape(32, 1), (4, 1))
    w_col = jnp.tile(weight.reshape(32, 1), (4, 1))
    return a_row, a_col, w_col, weight, skip_gain.reshape(GROUPS, WIDTH, 1)


GATE = ((GROUPS * WIDTH, LENGTH), BF16)
ARRIVED = ((SPANS, GROUPS * WIDTH, SPAN), BF16)
CAT = ((ROWS, 512), BF16)
TURN = ((GROUPS, 256, ROWS), BF16)
WHOLE = ((ROWS, 256), F32)
STATES = ((ROWS, 128), F32)
ENTER = ((ROWS + WIDTH + 8, 128), F32)
TOEP = ((GROUPS, 256, 256), BF16)
MATS = ((2, 128, 256), BF16)
PARTS = ((CTX, 16, 128), F32)
SMALL = ((2 * CTX + 1, 8, 128), F32)
RESIDUE = ((GROUPS, MODES), F32)
SKIP = ((1, GROUPS * WIDTH), F32)


def local(first, second, third, grad_out, exchange, residue, decay_rate, skip_gain, place):
    a_row, a_col, w_col, weight, skip = prepare(residue, decay_rate, skip_gain)
    outs = [CAT, TURN, WHOLE, ENTER, TOEP, MATS]
    x_cat, x_turn, conv, enter, back_toep, mats = call(
        forward_kernel,
        outs,
        [GATE, GATE] + outs + [STATES, TOEP],
        8,
        (first, second, a_row, a_col, w_col, decay_rate, weight, skip),
        vmem=(2, 3, 4, 7),
        smem=(5, 6),
    )
    payload, grad_out = call(
        middle_kernel,
        [PARTS, ARRIVED],
        [GATE, CAT, TURN, ENTER, CAT, STATES, PARTS],
        5 + len(RUNS),
        (grad_out, third, x_cat, x_turn, enter),
        vmem=(0,),
    )
    parts = exchange(payload)
    mixed, small = call(
        backward_kernel,
        [WHOLE, SMALL],
        [ARRIVED, GATE, TOEP, MATS, CAT, STATES, STATES, WHOLE, SMALL],
        6,
        (grad_out, third, back_toep, mats, a_row, skip, place, payload),
        vmem=(4, 5),
        smem=(6,),
    )
    outs = [GATE, GATE, GATE, RESIDUE, SKIP]
    grad_first, grad_second, grad_third, grad_residue, grad_skip = call(
        finish_kernel,
        outs,
        [SMALL, MATS, WHOLE, WHOLE, ARRIVED, GATE, GATE] + outs + [((2, SPANS, 128), F32)],
        FINISH_COPIES,
        (parts, small, mats, conv, mixed, grad_out, first, second),
        vmem=(0,),
    )
    return grad_first, grad_second, grad_third, grad_residue, grad_skip.reshape(GROUPS * WIDTH)


def on_device(first, second, third, grad_heads, residue, decay_rate, skip_gain):
    grad_out = lax.all_to_all(
        swap(grad_heads.reshape(SPANS, GROUPS * WIDTH, SPAN)),
        "ch",
        split_axis=0,
        concat_axis=0,
        tiled=True,
        axis_index_groups=[CH_ORDER],
    )
    place = lax.axis_index("ctx").astype(jnp.int32).reshape(1)

    def exchange(payload):
        return lax.all_to_all(
            payload, "ctx", split_axis=0, concat_axis=0, tiled=True, axis_index_groups=[CTX_ORDER]
        )

    return local(first, second, third, grad_out, exchange, residue, decay_rate, skip_gain, place)


def solution(mesh):
    return jax.shard_map(
        on_device,
        mesh=mesh,
        in_specs=(
            P("ch", "ctx"),
            P("ch", "ctx"),
            P("ch", "ctx"),
            P(None, ("ctx", "ch")),
            P("ch", None),
            P("ch", None),
            P("ch"),
        ),
        out_specs=(P("ch", "ctx"), P("ch", "ctx"), P("ch", "ctx"), P("ch", None), P("ch")),
        check_vma=False,
    )
```

```python
import jax
import jax.numpy as jnp
from jax import lax
from jax.experimental import pallas as pl
from jax.experimental.pallas import tpu as pltpu
from jax.sharding import PartitionSpec as P

F32, BF16 = jnp.float32, jnp.bfloat16
SPAN = 128
SPANS = 64
GROUPS, WIDTH, MODES = 2, 16, 16
ROWS = SPANS * WIDTH
LENGTH = SPAN * SPANS
CTX = 8
TOKENS = LENGTH * CTX


def iota(shape, dim):
    return lax.broadcasted_iota(jnp.int32, shape, dim)


def high(x):
    return x.astype(BF16)


def low(x):
    return (x - x.astype(BF16).astype(F32)).astype(BF16)


def dot(a, b):
    return jnp.dot(a, b, preferred_element_type=F32)


def halves(x):
    return x[:, :128] + x[:, 128:]


def state_matrix(a_row, age):
    decay = jnp.exp(-a_row * age)
    lane_group = (iota((128, 128), 1) % 32) // MODES
    out = []
    for g in range(GROUPS):
        mine = jnp.where(lane_group == g, decay, 0.0)
        block = jnp.concatenate([high(mine), low(mine)], axis=1)
        out += [block, block]
    return jnp.concatenate(out, axis=0)


def mode_matrix(a_col, w_col, age):
    wave = w_col * jnp.exp(-a_col * age)
    row = iota((128, 128), 0)
    part = jnp.where(row < 64, wave.astype(BF16).astype(F32), low(wave).astype(F32))
    row_group = (row % 32) // MODES
    return jnp.concatenate(
        [jnp.where(row_group == g, part, 0.0).astype(BF16) for g in range(GROUPS)], axis=1
    )


def quad_split(x, lane):
    top = x.astype(BF16).astype(F32)
    return jnp.where((lane // 32) % 2 == 0, top, x - top).astype(BF16)


def toeplitz(a_s, w_s, g, gap):
    near = jnp.maximum(gap, 0).astype(F32)
    total = jnp.zeros((SPAN, SPAN), F32)
    for r in range(MODES):
        total = total + w_s[g, r] * jnp.exp(-a_s[g, r] * near)
    total = jnp.where(gap >= 0, total, 0.0)
    block = jnp.concatenate([high(total), low(total)], axis=1)
    return jnp.concatenate([block, block], axis=0)


def begin(pairs, sems, first=0):
    copies = [
        pltpu.make_async_copy(source, target, sems.at[first + i]) for i, (source, target) in enumerate(pairs)
    ]
    for copy in copies:
        copy.start()
    return copies


def finish(copies):
    for copy in copies:
        copy.wait()


def forward_kernel(
    first_hbm, second_hbm, third_hbm, a_row, a_col, w_col, a_s, w_s, skip,
    x_turn, enter, edge, third, x_cat_hbm, conv_hbm, back_toep_hbm, mats_hbm,
    first, second, x_cat, conv, back_toep, mats, states, toep, sems,
):
    inputs = begin([(first_hbm, first), (second_hbm, second)], sems)
    outputs = begin([(third_hbm, third)], sems, 6)
    a = a_row[...]
    row = iota((128, 128), 0)
    col = iota((128, 128), 1)
    token = row.astype(F32)
    lane_token = col.astype(F32)
    mats[0] = mode_matrix(a_col[...], w_col[...], lane_token)
    mats[1] = mode_matrix(a_col[...], w_col[...], 127.0 - lane_token)
    for g in range(GROUPS):
        toep[g] = toeplitz(a_s, w_s, g, col - row)
        back_toep[g] = toeplitz(a_s, w_s, g, row - col)
    outputs += begin([(back_toep, back_toep_hbm), (mats, mats_hbm)], sems, 2)
    finish(inputs)
    for n in range(SPANS):
        at, here = pl.ds(n * WIDTH, WIDTH), pl.ds(n * SPAN, SPAN)
        x = first[:, here].astype(F32) * second[:, here].astype(F32)
        hi, lo = high(x), low(x)
        for g in range(GROUPS):
            c = slice(g * WIDTH, (g + 1) * WIDTH)
            x_cat[at, pl.ds(256 * g, 128)] = hi[c]
            x_cat[at, pl.ds(256 * g + 128, 128)] = lo[c]
    outputs += begin([(x_cat, x_cat_hbm)], sems, 4)
    states[...] = halves(dot(x_cat[...], state_matrix(a, 128.0 - token)))
    step = jnp.exp(-a * 128.0)
    carry = jnp.zeros((WIDTH, 128), F32)
    lane = iota((WIDTH, 128), 1)
    for n in range(SPANS):
        at = pl.ds(n * WIDTH, WIDTH)
        enter[at, :] = quad_split(carry, lane)
        carry = carry * step + states[at, :]
    edge[:WIDTH, :] = carry
    edge[WIDTH:, :] = jnp.broadcast_to(a, (8, 128))
    conv[...] = dot(enter[...], mats[0])
    for g in range(GROUPS):
        mine = pl.ds(256 * g, 256)
        here = pl.ds(128 * g, 128)
        x = x_cat[:, mine]
        gain = jnp.concatenate([skip[g]] * SPANS, axis=0)
        gated = x[:, :128].astype(F32) + x[:, 128:].astype(F32)
        conv[:, here] = conv[:, here] + halves(dot(x, toep[g])) + gain * gated
        x_turn[g] = x.T
    outputs += begin([(conv, conv_hbm)], sems, 5)
    finish(outputs)


FIRST = 36
CH_ORDER = [FIRST if p == 0 else 0 if p == FIRST else p for p in range(SPANS)]
CTX_ORDER = [5, 1, 3, 7, 2, 0, 4, 6]
CTX_PLACE = [CTX_ORDER.index(k) for k in range(CTX)]
RUNS = [(0, 1)] + [(i, min(i + 5, FIRST)) for i in range(1, FIRST, 5)] + [(FIRST, FIRST + 1)]
RUNS += [(i, min(i + 5, SPANS)) for i in range(FIRST + 1, SPANS, 5)]


def swap_copies(source, target, sems, first=0):
    return begin(
        [
            (source.at[pl.ds(CH_ORDER[i], j - i)], target.at[pl.ds(i, j - i)])
            for i, j in RUNS
        ],
        sems,
        first,
    )


def swap_kernel(heads, swapped, sems):
    finish(swap_copies(heads, swapped, sems))


def swap(heads):
    return pl.pallas_call(
        swap_kernel,
        out_shape=pltpu.VMEM(heads.shape, heads.dtype),
        in_specs=[pl.BlockSpec(memory_space=pltpu.HBM)],
        out_specs=pl.BlockSpec(memory_space=pltpu.VMEM),
        scratch_shapes=[pltpu.SemaphoreType.DMA((len(RUNS),))],
    )(pltpu.with_memory_space_constraint(heads, pltpu.HBM))


def middle_kernel(
    grad_out, third, x_turn, enter, edge, x_cat_hbm,
    payload,
    x_cat, g_cat, states, sems,
):
    cat_in = begin([(x_cat_hbm, x_cat)], sems)
    row = iota((128, 128), 0)
    col = iota((128, 128), 1)
    token = row.astype(F32)
    for n in range(SPANS):
        at, here = pl.ds(n * WIDTH, WIDTH), pl.ds(n * SPAN, SPAN)
        y = grad_out[CH_ORDER[n]].astype(F32) * third[:, here].astype(F32)
        hi, lo = high(y), low(y)
        for g in range(GROUPS):
            c = slice(g * WIDTH, (g + 1) * WIDTH)
            g_cat[at, pl.ds(256 * g, 128)] = hi[c]
            g_cat[at, pl.ds(256 * g + 128, 128)] = lo[c]
    a = edge[WIDTH : WIDTH + 1, :]
    states[...] = halves(dot(g_cat[...], state_matrix(a, token + 1.0)))
    cross = []
    for g in range(GROUPS):
        four = dot(x_turn[g], g_cat[:, pl.ds(256 * g, 256)])
        four = halves(four[:128] + four[128:])
        four = jnp.where(col >= row, four, 0.0)
        cross += [high(four), low(four)]
    near = halves(dot(jnp.concatenate(cross, axis=1), state_matrix(a, token - 64.0)))
    near = near * jnp.exp(a * (token - 64.0))
    near = jnp.sum(near.reshape(16, 8, 128), axis=0)
    step = jnp.exp(-a * 128.0)
    carry = jnp.zeros((WIDTH, 128), F32)
    far = jnp.zeros((WIDTH, 128), F32)
    for n in reversed(range(SPANS)):
        at = pl.ds(n * WIDTH, WIDTH)
        now = states[at, :]
        far = far + now * enter[at, :].astype(F32)
        carry = carry * step + now
    far = far[:8] + far[8:]
    weight = near + (far + pltpu.roll(far, 32, 1)) * jnp.exp(a)
    finish(cat_in)
    total = []
    for g in range(GROUPS):
        mine = jnp.zeros((WIDTH, SPAN), F32)
        hi, lo = pl.ds(256 * g, 128), pl.ds(256 * g + 128, 128)
        for n in range(SPANS):
            at = pl.ds(n * WIDTH, WIDTH)
            x = x_cat[at, hi].astype(F32) + x_cat[at, lo].astype(F32)
            y = g_cat[at, hi].astype(F32) + g_cat[at, lo].astype(F32)
            mine = mine + x * y
        total.append(mine)
    direct = lax.dot_general(
        jnp.ones((8, SPAN), F32),
        jnp.concatenate(total * 4, axis=0),
        (((1,), (1,)), ((), ())),
        precision=lax.Precision.HIGHEST,
        preferred_element_type=F32,
    )
    quarter = iota((8, 128), 1) // 32
    back = jnp.where(
        quarter == 0, carry[:8], jnp.where(quarter == 1, carry[8:], jnp.where(quarter == 2, weight, direct))
    )
    ahead = jnp.where(quarter == 0, edge[0:8, :], edge[8:16, :])
    for k in range(CTX):
        payload[k, :8, :] = back
        payload[k, 8:, :] = ahead


def backward_kernel(
    grad_out, third, back_toep_hbm, mats_hbm, conv_hbm, a_row, skip, place, payload,
    mixed, small, mats, conv,
    back_toep, g_cat, states, leave, sems,
):
    mats_in, toep_in, conv_in = begin(
        [(mats_hbm, mats), (back_toep_hbm, back_toep), (conv_hbm, conv)], sems
    )
    a = a_row[...]
    token = iota((128, 128), 0).astype(F32)
    wide = jnp.broadcast_to(a, (8, 128)) * float(LENGTH)
    is_state = iota((8, 128), 1) < 64
    me = place[0]
    for k in range(CTX):
        after = jnp.maximum(k - me - 1, 0).astype(F32)
        before = jnp.maximum(me - 1 - k, 0).astype(F32)
        later = jnp.where(k > me, 1.0, 0.0)
        earlier = jnp.where(k < me, 1.0, 0.0)
        small[k] = jnp.where(is_state, jnp.exp(-wide * after) * later, 1.0)
        small[CTX + k] = jnp.exp(-wide * before) * earlier
    small[2 * CTX] = jnp.broadcast_to(a, (8, 128))
    for n in range(SPANS):
        at, here = pl.ds(n * WIDTH, WIDTH), pl.ds(n * SPAN, SPAN)
        y = grad_out[CH_ORDER[n]].astype(F32) * third[:, here].astype(F32)
        hi, lo = high(y), low(y)
        for g in range(GROUPS):
            c = slice(g * WIDTH, (g + 1) * WIDTH)
            g_cat[at, pl.ds(256 * g, 128)] = hi[c]
            g_cat[at, pl.ds(256 * g + 128, 128)] = lo[c]
    states[...] = halves(dot(g_cat[...], state_matrix(a, token + 1.0)))
    step = jnp.exp(-a * 128.0)
    carry = jnp.zeros((WIDTH, 128), F32)
    for n in reversed(range(SPANS)):
        at = pl.ds(n * WIDTH, WIDTH)
        leave[at, :] = carry
        carry = carry * step + states[at, :]
    lane = iota((ROWS, 128), 1)
    finish([mats_in])
    mixed[...] = dot(quad_split(leave[...], lane), mats[1])
    finish([toep_in])
    for g in range(GROUPS):
        here = pl.ds(128 * g, 128)
        y = g_cat[:, pl.ds(256 * g, 256)]
        gain = jnp.concatenate([skip[g]] * SPANS, axis=0)
        grad_conv = y[:, :128].astype(F32) + y[:, 128:].astype(F32)
        mixed[:, here] = mixed[:, here] + halves(dot(y, back_toep[g])) + gain * grad_conv
    finish([conv_in])


CHUNKS = 4
CHUNK_SPANS = SPANS // CHUNKS
CHUNK_ROWS = ROWS // CHUNKS
CHUNK_TOKENS = LENGTH // CHUNKS


def finish_kernel(
    parts, small, mats, conv, mixed, grad_out, first_hbm, second_hbm,
    grad_first_hbm, grad_second_hbm, grad_third_hbm, grad_residue_hbm, grad_skip_hbm,
    first, second, grad_first, grad_second, grad_third, grad_residue, grad_skip, decays,
    sems,
):
    def rows_of(c):
        return pl.ds(c * CHUNK_ROWS, CHUNK_ROWS)

    def spans_of(c):
        return pl.ds(c * CHUNK_SPANS, CHUNK_SPANS)

    def tokens_of(c):
        return pl.ds(c * CHUNK_TOKENS, CHUNK_TOKENS)

    gate_in = []
    for c in range(CHUNKS):
        gate_in.append(
            begin(
                [
                    (first_hbm.at[:, tokens_of(c)], first.at[:, tokens_of(c)]),
                    (second_hbm.at[:, tokens_of(c)], second.at[:, tokens_of(c)]),
                ],
                sems,
                2 * c,
            )
        )
    used = 2 * CHUNKS
    a = small[2 * CTX, 0:1, :]
    quarter = iota((8, 128), 1) // 32
    back = jnp.zeros((8, 128), F32)
    ahead = jnp.zeros((8, 128), F32)
    running = jnp.zeros((8, 128), F32)
    far = jnp.zeros((8, 128), F32)
    block_step = jnp.exp(-a * float(LENGTH))
    for k in range(CTX):
        at = CTX_PLACE[k]
        later, earlier = parts[at, :8, :], parts[at, 8:, :]
        back = back + later * small[k]
        ahead = ahead + earlier * small[CTX + k]
        far = far + later * running
        running = running * block_step + earlier

    def spread(x, q):
        x = jnp.where(quarter == q, x, 0.0)
        x = x + pltpu.roll(x, 32, 1)
        return x + pltpu.roll(x, 64, 1)

    def rows(x):
        return jnp.concatenate([spread(x, 0), spread(x, 1)], axis=0)

    span = iota((SPANS, 128), 0).astype(F32)
    decays[0] = jnp.exp(-a * (128.0 * span))
    decays[1] = jnp.exp(-a * (128.0 * (SPANS - 1.0 - span)))
    lane = iota((CHUNK_ROWS, 128), 1)

    def fix(x, side, c):
        decay = decays[side, spans_of(c), :].reshape(CHUNK_SPANS, 1, 128)
        whole = (decay * x.reshape(1, WIDTH, 128)).reshape(CHUNK_ROWS, 128)
        return dot(quad_split(whole, lane), mats[side])

    def channels(x, i):
        x = x[i * WIDTH : (i + 1) * WIDTH]
        return jnp.concatenate([x[:, :128], x[:, 128:]], axis=0)

    outputs = []
    entering, leaving = rows(ahead), rows(back)
    for c in range(CHUNKS):
        add = fix(entering, 0, c)
        full = conv[rows_of(c), :] + add
        for i in range(CHUNK_SPANS):
            n = c * CHUNK_SPANS + i
            grad_third[:, pl.ds(n * SPAN, SPAN)] = (grad_out[CH_ORDER[n]].astype(F32) * channels(full, i)).astype(BF16)
        outputs += begin([(grad_third.at[:, tokens_of(c)], grad_third_hbm.at[:, tokens_of(c)])], sems, used)
        used += 1
    near = spread(back, 2)
    crossed = (spread(far, 0) + spread(far, 1)) * jnp.exp(a)
    weight = jnp.sum(near + crossed, axis=0, keepdims=True)
    weight = weight * jnp.sqrt(2.0 * a) * (1.0 / (float(WIDTH * TOKENS) ** 0.5))
    grad_residue[0:1, :] = weight[:, :MODES]
    grad_residue[1:2, :] = pltpu.roll(weight, 128 - MODES, 1)[:, :MODES]
    direct = pltpu.roll(back, 32, 1)[0:1] * (1.0 / (float(TOKENS) ** 0.5))
    grad_skip[...] = direct[:, : GROUPS * WIDTH]
    outputs += begin([(grad_residue, grad_residue_hbm), (grad_skip, grad_skip_hbm)], sems, used)
    used += 2
    for c in range(CHUNKS):
        add = fix(leaving, 1, c)
        finish(gate_in[c])
        full = mixed[rows_of(c), :] + add
        for i in range(CHUNK_SPANS):
            here = pl.ds((c * CHUNK_SPANS + i) * SPAN, SPAN)
            part = channels(full, i)
            grad_first[:, here] = (part * second[:, here].astype(F32)).astype(BF16)
            grad_second[:, here] = (part * first[:, here].astype(F32)).astype(BF16)
        outputs += begin(
            [
                (grad_first.at[:, tokens_of(c)], grad_first_hbm.at[:, tokens_of(c)]),
                (grad_second.at[:, tokens_of(c)], grad_second_hbm.at[:, tokens_of(c)]),
            ],
            sems,
            used,
        )
        used += 2
    finish(outputs)


FINISH_COPIES = 2 * CHUNKS + 3 * CHUNKS + 2


def placed(kind, shape, dtype):
    return kind(shape, dtype)


def pin(x, kind):
    return pltpu.with_memory_space_constraint(x, kind)


def call(kernel, outs, scratch, copies, args, near=(), vmem=(), smem=(), outs_near=()):
    def space(i):
        return pltpu.VMEM if i in vmem or i in near else pltpu.SMEM if i in smem else pltpu.HBM

    def pinned(i, x):
        return x if i in vmem or i in smem else pin(x, space(i))

    kinds = [pltpu.VMEM if i in outs_near else pltpu.HBM for i in range(len(outs))]
    return pl.pallas_call(
        kernel,
        out_shape=tuple(placed(kind, s, d) for kind, (s, d) in zip(kinds, outs)),
        in_specs=[pl.BlockSpec(memory_space=space(i)) for i in range(len(args))],
        out_specs=tuple(pl.BlockSpec(memory_space=kind) for kind in kinds),
        scratch_shapes=[pltpu.VMEM(s, d) for s, d in scratch] + [pltpu.SemaphoreType.DMA((copies,))],
        compiler_params=pltpu.CompilerParams(vmem_limit_bytes=40 << 20),
    )(*(pinned(i, x) for i, x in enumerate(args)))


def prepare(residue, decay_rate, skip_gain):
    weight = residue * jnp.sqrt(2.0 * decay_rate)
    a_row = jnp.tile(decay_rate.reshape(1, 32), (1, 4))
    a_col = jnp.tile(decay_rate.reshape(32, 1), (4, 1))
    w_col = jnp.tile(weight.reshape(32, 1), (4, 1))
    return a_row, a_col, w_col, weight, skip_gain.reshape(GROUPS, WIDTH, 1)


GATE = ((GROUPS * WIDTH, LENGTH), BF16)
ARRIVED = ((SPANS, GROUPS * WIDTH, SPAN), BF16)
CAT = ((ROWS, 512), BF16)
TURN = ((GROUPS, 256, ROWS), BF16)
WHOLE = ((ROWS, 256), F32)
STATES = ((ROWS, 128), F32)
ENTER = ((ROWS, 128), BF16)
EDGE = ((WIDTH + 8, 128), F32)
TOEP = ((GROUPS, 256, 256), BF16)
MATS = ((2, 128, 256), BF16)
PARTS = ((CTX, 16, 128), F32)
SMALL = ((2 * CTX + 1, 8, 128), F32)
RESIDUE = ((GROUPS, MODES), F32)
SKIP = ((1, GROUPS * WIDTH), F32)


def local(first, second, third, grad_out, exchange, residue, decay_rate, skip_gain, place):
    a_row, a_col, w_col, weight, skip = prepare(residue, decay_rate, skip_gain)
    x_turn, enter, edge, third, x_cat, conv, back_toep, mats = call(
        forward_kernel,
        [TURN, ENTER, EDGE, GATE, CAT, WHOLE, TOEP, MATS],
        [GATE, GATE, CAT, WHOLE, TOEP, MATS, STATES, TOEP],
        7,
        (first, second, third, a_row, a_col, w_col, decay_rate, weight, skip),
        vmem=(3, 4, 5, 8),
        smem=(6, 7),
        outs_near=(0, 1, 2, 3),
    )
    (payload,) = call(
        middle_kernel,
        [PARTS],
        [CAT, CAT, STATES],
        1,
        (grad_out, third, x_turn, enter, edge, x_cat),
        near=(0, 1, 2, 3, 4),
        outs_near=(0,),
    )
    parts = exchange(payload)
    mixed, small, mats, conv = call(
        backward_kernel,
        [WHOLE, SMALL, MATS, WHOLE],
        [TOEP, CAT, STATES, STATES],
        3,
        (grad_out, third, back_toep, mats, conv, a_row, skip, place, payload),
        near=(0, 1, 8),
        vmem=(5, 6),
        smem=(7,),
        outs_near=(0, 1, 2, 3),
    )
    outs = [GATE, GATE, GATE, RESIDUE, SKIP]
    grad_first, grad_second, grad_third, grad_residue, grad_skip = call(
        finish_kernel,
        outs,
        [GATE, GATE] + outs + [((2, SPANS, 128), F32)],
        FINISH_COPIES,
        (parts, small, mats, conv, mixed, grad_out, first, second),
        near=(0, 1, 2, 3, 4, 5),
    )
    return grad_first, grad_second, grad_third, grad_residue, grad_skip.reshape(GROUPS * WIDTH)


def on_device(first, second, third, grad_heads, residue, decay_rate, skip_gain):
    grad_out = lax.all_to_all(
        swap(grad_heads.reshape(SPANS, GROUPS * WIDTH, SPAN)),
        "ch",
        split_axis=0,
        concat_axis=0,
        tiled=True,
        axis_index_groups=[CH_ORDER],
    )
    place = lax.axis_index("ctx").astype(jnp.int32).reshape(1)

    def exchange(payload):
        return lax.all_to_all(
            payload, "ctx", split_axis=0, concat_axis=0, tiled=True, axis_index_groups=[CTX_ORDER]
        )

    return local(first, second, third, grad_out, exchange, residue, decay_rate, skip_gain, place)


def solution(mesh):
    return jax.shard_map(
        on_device,
        mesh=mesh,
        in_specs=(
            P("ch", "ctx"),
            P("ch", "ctx"),
            P("ch", "ctx"),
            P(None, ("ctx", "ch")),
            P("ch", None),
            P("ch", None),
            P("ch"),
        ),
        out_specs=(P("ch", "ctx"), P("ch", "ctx"), P("ch", "ctx"), P("ch", None), P("ch")),
        check_vma=False,
    )
```

```python
import jax
import jax.numpy as jnp
from jax import lax
from jax.experimental import pallas as pl
from jax.experimental.pallas import tpu as pltpu
from jax.sharding import PartitionSpec as P

F32, BF16 = jnp.float32, jnp.bfloat16
SPAN = 128
SPANS = 64
GROUPS, WIDTH, MODES = 2, 16, 16
ROWS = SPANS * WIDTH
LENGTH = SPAN * SPANS
CTX = 8
TOKENS = LENGTH * CTX


def iota(shape, dim):
    return lax.broadcasted_iota(jnp.int32, shape, dim)


def high(x):
    return x.astype(BF16)


def low(x):
    return (x - x.astype(BF16).astype(F32)).astype(BF16)


def dot(a, b):
    return jnp.dot(a, b, preferred_element_type=F32)


def halves(x):
    return x[:, :128] + x[:, 128:]


def state_matrix(a_row, age):
    decay = jnp.exp(-a_row * age)
    lane_group = (iota((128, 128), 1) % 32) // MODES
    out = []
    for g in range(GROUPS):
        mine = jnp.where(lane_group == g, decay, 0.0)
        block = jnp.concatenate([high(mine), low(mine)], axis=1)
        out += [block, block]
    return jnp.concatenate(out, axis=0)


def mode_matrix(a_col, w_col, age):
    wave = w_col * jnp.exp(-a_col * age)
    row = iota((128, 128), 0)
    part = jnp.where(row < 64, wave.astype(BF16).astype(F32), low(wave).astype(F32))
    row_group = (row % 32) // MODES
    return jnp.concatenate(
        [jnp.where(row_group == g, part, 0.0).astype(BF16) for g in range(GROUPS)], axis=1
    )


def quad_split(x, lane):
    top = x.astype(BF16).astype(F32)
    return jnp.where((lane // 32) % 2 == 0, top, x - top).astype(BF16)


def toeplitz(a_s, w_s, g, gap):
    near = jnp.maximum(gap, 0).astype(F32)
    total = jnp.zeros((SPAN, SPAN), F32)
    for r in range(MODES):
        total = total + w_s[g, r] * jnp.exp(-a_s[g, r] * near)
    total = jnp.where(gap >= 0, total, 0.0)
    block = jnp.concatenate([high(total), low(total)], axis=1)
    return jnp.concatenate([block, block], axis=0)


def begin(pairs, sems, first=0):
    copies = [
        pltpu.make_async_copy(source, target, sems.at[first + i]) for i, (source, target) in enumerate(pairs)
    ]
    for copy in copies:
        copy.start()
    return copies


def finish(copies):
    for copy in copies:
        copy.wait()


def forward_kernel(
    first_hbm, second_hbm, third_hbm, a_row, a_col, w_col, a_s, w_s, skip,
    x_turn, edge, third, gated, pairs, conv_hbm, back_toep_hbm, mats_hbm,
    first, second, x_cat, enter, conv, back_toep, mats, states, toep, sems,
):
    inputs = begin([(first_hbm, first), (second_hbm, second)], sems)
    outputs = begin([(third_hbm, third)], sems, 5)
    a = a_row[...]
    row = iota((128, 128), 0)
    col = iota((128, 128), 1)
    token = row.astype(F32)
    lane_token = col.astype(F32)
    mats[0] = mode_matrix(a_col[...], w_col[...], lane_token)
    mats[1] = mode_matrix(a_col[...], w_col[...], 127.0 - lane_token)
    for g in range(GROUPS):
        toep[g] = toeplitz(a_s, w_s, g, col - row)
        back_toep[g] = toeplitz(a_s, w_s, g, row - col)
    outputs += begin([(back_toep, back_toep_hbm), (mats, mats_hbm)], sems, 2)
    finish(inputs)
    for n in range(SPANS):
        at, here = pl.ds(n * WIDTH, WIDTH), pl.ds(n * SPAN, SPAN)
        x = first[:, here].astype(F32) * second[:, here].astype(F32)
        hi, lo = high(x), low(x)
        for g in range(GROUPS):
            c = slice(g * WIDTH, (g + 1) * WIDTH)
            gated[at, pl.ds(128 * g, 128)] = x[c]
            x_cat[at, pl.ds(256 * g, 128)] = hi[c]
            x_cat[at, pl.ds(256 * g + 128, 128)] = lo[c]
    states[...] = halves(dot(x_cat[...], state_matrix(a, 128.0 - token)))
    step = jnp.exp(-a * 128.0)
    carry = jnp.zeros((WIDTH, 128), F32)
    lane = iota((WIDTH, 128), 1)
    for n in range(SPANS):
        at = pl.ds(n * WIDTH, WIDTH)
        enter[at, :] = quad_split(carry, lane)
        carry = carry * step + states[at, :]
    edge[:WIDTH, :] = carry
    edge[WIDTH:, :] = jnp.broadcast_to(a, (8, 128))
    odd = iota((WIDTH, 128), 1) >= 64
    for n in range(0, SPANS, 2):
        even_rows, odd_rows = enter[pl.ds(n * WIDTH, WIDTH), :], enter[pl.ds((n + 1) * WIDTH, WIDTH), :]
        pairs[pl.ds(n * WIDTH // 2, WIDTH), :] = jnp.where(
            odd, odd_rows.astype(F32), even_rows.astype(F32)
        ).astype(BF16)
    conv[...] = dot(enter[...], mats[0])
    for g in range(GROUPS):
        mine = pl.ds(256 * g, 256)
        here = pl.ds(128 * g, 128)
        x = x_cat[:, mine]
        gain = jnp.concatenate([skip[g]] * SPANS, axis=0)
        conv[:, here] = conv[:, here] + halves(dot(x, toep[g])) + gain * gated[:, here]
        x_turn[g] = x.T
    outputs += begin([(conv, conv_hbm)], sems, 4)
    finish(outputs)


FIRST = 45
CH_ORDER = [FIRST if p == 0 else 0 if p == FIRST else p for p in range(SPANS)]
CTX_ORDER = [5, 1, 3, 7, 2, 0, 4, 6]
CTX_PLACE = [CTX_ORDER.index(k) for k in range(CTX)]
RUNS = [(0, 1), (FIRST, FIRST + 1)]
RUNS += [(i, min(i + 9, FIRST)) for i in range(1, FIRST, 9)]
RUNS += [(i, min(i + 9, SPANS)) for i in range(FIRST + 1, SPANS, 9)]


def swap_kernel(heads, swapped, held, sems):
    arriving = begin(
        [(heads.at[pl.ds(CH_ORDER[i], j - i)], held.at[pl.ds(i, j - i)]) for i, j in RUNS], sems
    )
    leaving = []
    for r, (i, j) in enumerate(RUNS):
        finish([arriving[r]])
        leaving += begin([(held.at[pl.ds(i, j - i)], swapped.at[pl.ds(i, j - i)])], sems, len(RUNS) + r)
    finish(leaving)


def swap(heads):
    (swapped,) = call(swap_kernel, [ARRIVED], [ARRIVED], 2 * len(RUNS), (heads,))
    return swapped


def middle_kernel(
    grad_out, third, x_turn, edge, gated, pairs,
    payload, states_hbm,
    g_cat, states, sems,
):
    row = iota((128, 128), 0)
    col = iota((128, 128), 1)
    token = row.astype(F32)
    total = [jnp.zeros((WIDTH, SPAN), F32) for _ in range(GROUPS)]
    for n in range(SPANS):
        at, here = pl.ds(n * WIDTH, WIDTH), pl.ds(n * SPAN, SPAN)
        y = grad_out[CH_ORDER[n]].astype(F32) * third[:, here].astype(F32)
        hi, lo = high(y), low(y)
        for g in range(GROUPS):
            c = slice(g * WIDTH, (g + 1) * WIDTH)
            g_cat[at, pl.ds(256 * g, 128)] = hi[c]
            g_cat[at, pl.ds(256 * g + 128, 128)] = lo[c]
            total[g] = total[g] + y[c] * gated[at, pl.ds(128 * g, 128)]
    a = edge[WIDTH : WIDTH + 1, :]
    states[...] = halves(dot(g_cat[...], state_matrix(a, token + 1.0)))
    outputs = begin([(states, states_hbm)], sems)
    cross = []
    for g in range(GROUPS):
        four = dot(x_turn[g], g_cat[:, pl.ds(256 * g, 256)])
        four = halves(four[:128] + four[128:])
        four = jnp.where(col >= row, four, 0.0)
        cross += [high(four), low(four)]
    near = halves(dot(jnp.concatenate(cross, axis=1), state_matrix(a, token - 64.0)))
    near = near * jnp.exp(a * (token - 64.0))
    near = jnp.sum(near.reshape(16, 8, 128), axis=0)
    step = jnp.exp(-a * 128.0)
    carry = jnp.zeros((WIDTH, 128), F32)
    far = jnp.zeros((WIDTH, 128), F32)
    odd = iota((WIDTH, 128), 1) >= 64
    for n in reversed(range(0, SPANS, 2)):
        later, earlier = states[pl.ds((n + 1) * WIDTH, WIDTH), :], states[pl.ds(n * WIDTH, WIDTH), :]
        far = far + jnp.where(odd, later, earlier) * pairs[pl.ds(n * WIDTH // 2, WIDTH), :].astype(F32)
        carry = (carry * step + later) * step + earlier
    far = far[:8] + far[8:]
    far = far + pltpu.roll(far, 32, 1)
    weight = near + (far + pltpu.roll(far, 64, 1)) * jnp.exp(a)
    direct = lax.dot_general(
        jnp.ones((8, SPAN), F32),
        jnp.concatenate(total * 4, axis=0),
        (((1,), (1,)), ((), ())),
        precision=lax.Precision.HIGHEST,
        preferred_element_type=F32,
    )
    quarter = iota((8, 128), 1) // 32
    back = jnp.where(
        quarter == 0, carry[:8], jnp.where(quarter == 1, carry[8:], jnp.where(quarter == 2, weight, direct))
    )
    ahead = jnp.where(quarter == 0, edge[0:8, :], edge[8:16, :])
    for k in range(CTX):
        payload[k, :8, :] = back
        payload[k, 8:, :] = ahead
    finish(outputs)


def backward_kernel(
    grad_out, third, states_hbm, back_toep_hbm, mats_hbm, conv_hbm, a_row, skip, place,
    mixed, small, mats, conv,
    g_cat, states, back_toep, leave, sems,
):
    states_in, mats_in, toep_in, conv_in = begin(
        [(states_hbm, states), (mats_hbm, mats), (back_toep_hbm, back_toep), (conv_hbm, conv)], sems
    )
    a = a_row[...]
    wide = jnp.broadcast_to(a, (8, 128)) * float(LENGTH)
    is_state = iota((8, 128), 1) < 64
    me = place[0]
    for k in range(CTX):
        after = jnp.maximum(k - me - 1, 0).astype(F32)
        before = jnp.maximum(me - 1 - k, 0).astype(F32)
        later = jnp.where(k > me, 1.0, 0.0)
        earlier = jnp.where(k < me, 1.0, 0.0)
        small[k] = jnp.where(is_state, jnp.exp(-wide * after) * later, 1.0)
        small[CTX + k] = jnp.exp(-wide * before) * earlier
    small[2 * CTX] = jnp.broadcast_to(a, (8, 128))
    for n in range(SPANS):
        at, here = pl.ds(n * WIDTH, WIDTH), pl.ds(n * SPAN, SPAN)
        y = grad_out[CH_ORDER[n]].astype(F32) * third[:, here].astype(F32)
        hi, lo = high(y), low(y)
        for g in range(GROUPS):
            c = slice(g * WIDTH, (g + 1) * WIDTH)
            g_cat[at, pl.ds(256 * g, 128)] = hi[c]
            g_cat[at, pl.ds(256 * g + 128, 128)] = lo[c]
    lane = iota((WIDTH, 128), 1)
    finish([states_in])
    step = jnp.exp(-a * 128.0)
    carry = jnp.zeros((WIDTH, 128), F32)
    for n in reversed(range(SPANS)):
        at = pl.ds(n * WIDTH, WIDTH)
        leave[at, :] = quad_split(carry, lane)
        carry = carry * step + states[at, :]
    finish([mats_in])
    mixed[...] = dot(leave[...], mats[1])
    finish([toep_in])
    for g in range(GROUPS):
        here = pl.ds(128 * g, 128)
        y = g_cat[:, pl.ds(256 * g, 256)]
        gain = jnp.concatenate([skip[g]] * SPANS, axis=0)
        grad_conv = y[:, :128].astype(F32) + y[:, 128:].astype(F32)
        mixed[:, here] = mixed[:, here] + halves(dot(y, back_toep[g])) + gain * grad_conv
    finish([conv_in])


CHUNKS = 4
CHUNK_SPANS = SPANS // CHUNKS
CHUNK_ROWS = ROWS // CHUNKS
CHUNK_TOKENS = LENGTH // CHUNKS


def finish_kernel(
    parts, small, mats, conv, mixed, grad_out, first_hbm, second_hbm,
    grad_first_hbm, grad_second_hbm, grad_third_hbm, grad_residue_hbm, grad_skip_hbm,
    first, second, grad_first, grad_second, grad_third, grad_residue, grad_skip, decays,
    sems,
):
    def rows_of(c):
        return pl.ds(c * CHUNK_ROWS, CHUNK_ROWS)

    def spans_of(c):
        return pl.ds(c * CHUNK_SPANS, CHUNK_SPANS)

    def tokens_of(c):
        return pl.ds(c * CHUNK_TOKENS, CHUNK_TOKENS)

    gate_in = []
    for c in range(CHUNKS):
        gate_in.append(
            begin(
                [
                    (first_hbm.at[:, tokens_of(c)], first.at[:, tokens_of(c)]),
                    (second_hbm.at[:, tokens_of(c)], second.at[:, tokens_of(c)]),
                ],
                sems,
                2 * c,
            )
        )
    used = 2 * CHUNKS
    a = small[2 * CTX, 0:1, :]
    quarter = iota((8, 128), 1) // 32
    back = jnp.zeros((8, 128), F32)
    ahead = jnp.zeros((8, 128), F32)
    running = jnp.zeros((8, 128), F32)
    far = jnp.zeros((8, 128), F32)
    block_step = jnp.exp(-a * float(LENGTH))
    for k in range(CTX):
        at = CTX_PLACE[k]
        later, earlier = parts[at, :8, :], parts[at, 8:, :]
        back = back + later * small[k]
        ahead = ahead + earlier * small[CTX + k]
        far = far + later * running
        running = running * block_step + earlier

    def spread(x, q):
        x = jnp.where(quarter == q, x, 0.0)
        x = x + pltpu.roll(x, 32, 1)
        return x + pltpu.roll(x, 64, 1)

    def rows(x):
        return jnp.concatenate([spread(x, 0), spread(x, 1)], axis=0)

    span = iota((SPANS, 128), 0).astype(F32)
    decays[0] = jnp.exp(-a * (128.0 * span))
    decays[1] = jnp.exp(-a * (128.0 * (SPANS - 1.0 - span)))
    lane = iota((CHUNK_ROWS, 128), 1)

    def fix(x, side, c):
        decay = decays[side, spans_of(c), :].reshape(CHUNK_SPANS, 1, 128)
        whole = (decay * x.reshape(1, WIDTH, 128)).reshape(CHUNK_ROWS, 128)
        return dot(quad_split(whole, lane), mats[side])

    def channels(x, i):
        x = x[i * WIDTH : (i + 1) * WIDTH]
        return jnp.concatenate([x[:, :128], x[:, 128:]], axis=0)

    outputs = []
    entering, leaving = rows(ahead), rows(back)
    for c in range(CHUNKS):
        add = fix(entering, 0, c)
        full = conv[rows_of(c), :] + add
        for i in range(CHUNK_SPANS):
            n = c * CHUNK_SPANS + i
            grad_third[:, pl.ds(n * SPAN, SPAN)] = (grad_out[CH_ORDER[n]].astype(F32) * channels(full, i)).astype(BF16)
        outputs += begin([(grad_third.at[:, tokens_of(c)], grad_third_hbm.at[:, tokens_of(c)])], sems, used)
        used += 1
    near = spread(back, 2)
    crossed = (spread(far, 0) + spread(far, 1)) * jnp.exp(a)
    weight = jnp.sum(near + crossed, axis=0, keepdims=True)
    weight = weight * jnp.sqrt(2.0 * a) * (1.0 / (float(WIDTH * TOKENS) ** 0.5))
    grad_residue[0:1, :] = weight[:, :MODES]
    grad_residue[1:2, :] = pltpu.roll(weight, 128 - MODES, 1)[:, :MODES]
    direct = pltpu.roll(back, 32, 1)[0:1] * (1.0 / (float(TOKENS) ** 0.5))
    grad_skip[...] = direct[:, : GROUPS * WIDTH]
    outputs += begin([(grad_residue, grad_residue_hbm), (grad_skip, grad_skip_hbm)], sems, used)
    used += 2
    for c in range(CHUNKS):
        add = fix(leaving, 1, c)
        finish(gate_in[c])
        full = mixed[rows_of(c), :] + add
        for i in range(CHUNK_SPANS):
            here = pl.ds((c * CHUNK_SPANS + i) * SPAN, SPAN)
            part = channels(full, i)
            grad_first[:, here] = (part * second[:, here].astype(F32)).astype(BF16)
            grad_second[:, here] = (part * first[:, here].astype(F32)).astype(BF16)
        outputs += begin(
            [
                (grad_first.at[:, tokens_of(c)], grad_first_hbm.at[:, tokens_of(c)]),
                (grad_second.at[:, tokens_of(c)], grad_second_hbm.at[:, tokens_of(c)]),
            ],
            sems,
            used,
        )
        used += 2
    finish(outputs)


FINISH_COPIES = 2 * CHUNKS + 3 * CHUNKS + 2


def placed(kind, shape, dtype):
    return kind(shape, dtype)


def pin(x, kind):
    return pltpu.with_memory_space_constraint(x, kind)


def call(kernel, outs, scratch, copies, args, near=(), vmem=(), smem=(), outs_near=()):
    def space(i):
        return pltpu.VMEM if i in vmem or i in near else pltpu.SMEM if i in smem else pltpu.HBM

    def pinned(i, x):
        return x if i in vmem or i in smem else pin(x, space(i))

    kinds = [pltpu.VMEM if i in outs_near else pltpu.HBM for i in range(len(outs))]
    return pl.pallas_call(
        kernel,
        out_shape=tuple(placed(kind, s, d) for kind, (s, d) in zip(kinds, outs)),
        in_specs=[pl.BlockSpec(memory_space=space(i)) for i in range(len(args))],
        out_specs=tuple(pl.BlockSpec(memory_space=kind) for kind in kinds),
        scratch_shapes=[pltpu.VMEM(s, d) for s, d in scratch]
        + [pltpu.SemaphoreType.DMA((copies,))] * (copies > 0),
        compiler_params=pltpu.CompilerParams(vmem_limit_bytes=40 << 20),
    )(*(pinned(i, x) for i, x in enumerate(args)))


def prepare(residue, decay_rate, skip_gain):
    weight = residue * jnp.sqrt(2.0 * decay_rate)
    a_row = jnp.tile(decay_rate.reshape(1, 32), (1, 4))
    a_col = jnp.tile(decay_rate.reshape(32, 1), (4, 1))
    w_col = jnp.tile(weight.reshape(32, 1), (4, 1))
    return a_row, a_col, w_col, weight, skip_gain.reshape(GROUPS, WIDTH, 1)


GATE = ((GROUPS * WIDTH, LENGTH), BF16)
ARRIVED = ((SPANS, GROUPS * WIDTH, SPAN), BF16)
CAT = ((ROWS, 512), BF16)
TURN = ((GROUPS, 256, ROWS), BF16)
WHOLE = ((ROWS, 256), F32)
STATES = ((ROWS, 128), F32)
ENTER = ((ROWS, 128), BF16)
PAIRS = ((ROWS // 2, 128), BF16)
EDGE = ((WIDTH + 8, 128), F32)
TOEP = ((GROUPS, 256, 256), BF16)
MATS = ((2, 128, 256), BF16)
PARTS = ((CTX, 16, 128), F32)
SMALL = ((2 * CTX + 1, 8, 128), F32)
DECAYS = ((2, SPANS, 128), F32)
RESIDUE = ((GROUPS, MODES), F32)
SKIP = ((1, GROUPS * WIDTH), F32)


def local(first, second, third, grad_out, exchange, residue, decay_rate, skip_gain, place):
    a_row, a_col, w_col, weight, skip = prepare(residue, decay_rate, skip_gain)
    x_turn, edge, third, gated, pairs, conv, back_toep, mats = call(
        forward_kernel,
        [TURN, EDGE, GATE, WHOLE, PAIRS, WHOLE, TOEP, MATS],
        [GATE, GATE, CAT, ENTER, WHOLE, TOEP, MATS, STATES, TOEP],
        6,
        (first, second, third, a_row, a_col, w_col, decay_rate, weight, skip),
        vmem=(3, 4, 5, 8),
        smem=(6, 7),
        outs_near=(0, 1, 2, 3, 4),
    )
    payload, states = call(
        middle_kernel,
        [PARTS, STATES],
        [CAT, STATES],
        1,
        (grad_out, third, x_turn, edge, gated, pairs),
        near=(0, 1, 2, 3, 4, 5),
        outs_near=(0,),
    )
    parts = exchange(payload)
    mixed, small, mats, conv = call(
        backward_kernel,
        [WHOLE, SMALL, MATS, WHOLE],
        [CAT, STATES, TOEP, ENTER],
        4,
        (grad_out, third, states, back_toep, mats, conv, a_row, skip, place),
        near=(0, 1),
        vmem=(6, 7),
        smem=(8,),
        outs_near=(0, 1, 2, 3),
    )
    outs = [GATE, GATE, GATE, RESIDUE, SKIP]
    grad_first, grad_second, grad_third, grad_residue, grad_skip = call(
        finish_kernel,
        outs,
        [GATE, GATE] + outs + [DECAYS],
        FINISH_COPIES,
        (parts, small, mats, conv, mixed, grad_out, first, second),
        near=(0, 1, 2, 3, 4, 5),
    )
    return grad_first, grad_second, grad_third, grad_residue, grad_skip.reshape(GROUPS * WIDTH)


def on_device(first, second, third, grad_heads, residue, decay_rate, skip_gain):
    grad_out = lax.all_to_all(
        swap(grad_heads.reshape(SPANS, GROUPS * WIDTH, SPAN)),
        "ch",
        split_axis=0,
        concat_axis=0,
        tiled=True,
        axis_index_groups=[CH_ORDER],
    )
    place = lax.axis_index("ctx").astype(jnp.int32).reshape(1)

    def exchange(payload):
        return lax.all_to_all(
            payload, "ctx", split_axis=0, concat_axis=0, tiled=True, axis_index_groups=[CTX_ORDER]
        )

    return local(first, second, third, grad_out, exchange, residue, decay_rate, skip_gain, place)


def solution(mesh):
    return jax.shard_map(
        on_device,
        mesh=mesh,
        in_specs=(
            P("ch", "ctx"),
            P("ch", "ctx"),
            P("ch", "ctx"),
            P(None, ("ctx", "ch")),
            P("ch", None),
            P("ch", None),
            P("ch"),
        ),
        out_specs=(P("ch", "ctx"), P("ch", "ctx"), P("ch", "ctx"), P("ch", None), P("ch")),
        check_vma=False,
    )
```

```python
import jax
import jax.numpy as jnp
from jax import lax
from jax.experimental import pallas as pl
from jax.experimental.pallas import tpu as pltpu
from jax.sharding import PartitionSpec as P

F32, BF16 = jnp.float32, jnp.bfloat16
SPAN = 128
SPANS = 64
GROUPS, WIDTH, MODES = 2, 16, 16
ROWS = SPANS * WIDTH
LENGTH = SPAN * SPANS
CTX = 8
TOKENS = LENGTH * CTX


def iota(shape, dim):
    return lax.broadcasted_iota(jnp.int32, shape, dim)


def high(x):
    return x.astype(BF16)


def low(x):
    return (x - x.astype(BF16).astype(F32)).astype(BF16)


def dot(a, b):
    return jnp.dot(a, b, preferred_element_type=F32)


def halves(x):
    return x[:, :128] + x[:, 128:]


def state_matrix(a_row, age):
    decay = jnp.exp(-a_row * age)
    lane_group = (iota((128, 128), 1) % 32) // MODES
    out = []
    for g in range(GROUPS):
        mine = jnp.where(lane_group == g, decay, 0.0)
        block = jnp.concatenate([high(mine), low(mine)], axis=1)
        out += [block, block]
    return jnp.concatenate(out, axis=0)


def mode_matrix(a_col, w_col, age):
    wave = w_col * jnp.exp(-a_col * age)
    row = iota((128, 128), 0)
    part = jnp.where(row < 64, wave.astype(BF16).astype(F32), low(wave).astype(F32))
    row_group = (row % 32) // MODES
    return jnp.concatenate(
        [jnp.where(row_group == g, part, 0.0).astype(BF16) for g in range(GROUPS)], axis=1
    )


def quad_split(x, lane):
    top = x.astype(BF16).astype(F32)
    return jnp.where((lane // 32) % 2 == 0, top, x - top).astype(BF16)


def toeplitz(a_s, w_s, g, gap):
    near = jnp.maximum(gap, 0).astype(F32)
    total = jnp.zeros((SPAN, SPAN), F32)
    for r in range(MODES):
        total = total + w_s[g, r] * jnp.exp(-a_s[g, r] * near)
    total = jnp.where(gap >= 0, total, 0.0)
    block = jnp.concatenate([high(total), low(total)], axis=1)
    return jnp.concatenate([block, block], axis=0)


def begin(pairs, sems, first=0):
    copies = [
        pltpu.make_async_copy(source, target, sems.at[first + i]) for i, (source, target) in enumerate(pairs)
    ]
    for copy in copies:
        copy.start()
    return copies


def finish(copies):
    for copy in copies:
        copy.wait()


def forward_kernel(
    first_hbm, second_hbm, third_hbm, a_row, a_col, w_col, a_s, w_s, skip,
    x_turn, edge, third, gated, pairs, conv_hbm, back_toep_hbm, mats_hbm,
    first, second, x_cat, enter, conv, back_toep, mats, states, toep, sems,
):
    inputs = begin([(first_hbm, first), (second_hbm, second)], sems)
    outputs = begin([(third_hbm, third)], sems, 5)
    a = a_row[...]
    row = iota((128, 128), 0)
    col = iota((128, 128), 1)
    token = row.astype(F32)
    lane_token = col.astype(F32)
    mats[0] = mode_matrix(a_col[...], w_col[...], lane_token)
    mats[1] = mode_matrix(a_col[...], w_col[...], 127.0 - lane_token)
    for g in range(GROUPS):
        toep[g] = toeplitz(a_s, w_s, g, col - row)
        back_toep[g] = toeplitz(a_s, w_s, g, row - col)
    outputs += begin([(back_toep, back_toep_hbm), (mats, mats_hbm)], sems, 2)
    finish(inputs)
    for n in range(SPANS):
        at, here = pl.ds(n * WIDTH, WIDTH), pl.ds(n * SPAN, SPAN)
        x = first[:, here].astype(F32) * second[:, here].astype(F32)
        hi, lo = high(x), low(x)
        for g in range(GROUPS):
            c = slice(g * WIDTH, (g + 1) * WIDTH)
            gated[at, pl.ds(128 * g, 128)] = x[c]
            x_cat[at, pl.ds(256 * g, 128)] = hi[c]
            x_cat[at, pl.ds(256 * g + 128, 128)] = lo[c]
    states[...] = halves(dot(x_cat[...], state_matrix(a, 128.0 - token)))
    step = jnp.exp(-a * 128.0)
    carry = jnp.zeros((WIDTH, 128), F32)
    lane = iota((WIDTH, 128), 1)
    for n in range(SPANS):
        at = pl.ds(n * WIDTH, WIDTH)
        enter[at, :] = quad_split(carry, lane)
        carry = carry * step + states[at, :]
    edge[:WIDTH, :] = carry
    edge[WIDTH:, :] = jnp.broadcast_to(a, (8, 128))
    odd = iota((WIDTH, 128), 1) >= 64
    for n in range(0, SPANS, 2):
        even_rows, odd_rows = enter[pl.ds(n * WIDTH, WIDTH), :], enter[pl.ds((n + 1) * WIDTH, WIDTH), :]
        pairs[pl.ds(n * WIDTH // 2, WIDTH), :] = jnp.where(
            odd, odd_rows.astype(F32), even_rows.astype(F32)
        ).astype(BF16)
    conv[...] = dot(enter[...], mats[0])
    for g in range(GROUPS):
        mine = pl.ds(256 * g, 256)
        here = pl.ds(128 * g, 128)
        x = x_cat[:, mine]
        gain = jnp.concatenate([skip[g]] * SPANS, axis=0)
        conv[:, here] = conv[:, here] + halves(dot(x, toep[g])) + gain * gated[:, here]
        x_turn[g] = x.T
    outputs += begin([(conv, conv_hbm)], sems, 4)
    finish(outputs)


FIRST = 45
CH_ORDER = [FIRST if p == 0 else 0 if p == FIRST else p for p in range(SPANS)]
CTX_ORDER = [5, 1, 3, 7, 2, 0, 4, 6]
CTX_PLACE = [CTX_ORDER.index(k) for k in range(CTX)]
RUNS = [(0, 1), (FIRST, FIRST + 1)]
RUNS += [(i, min(i + 22, FIRST)) for i in range(1, FIRST, 22)]
RUNS += [(i, min(i + 22, SPANS)) for i in range(FIRST + 1, SPANS, 22)]


def swap_kernel(heads, swapped, held, sems):
    arriving = begin(
        [(heads.at[pl.ds(CH_ORDER[i], j - i)], held.at[pl.ds(i, j - i)]) for i, j in RUNS], sems
    )
    leaving = []
    for r, (i, j) in enumerate(RUNS):
        finish([arriving[r]])
        leaving += begin([(held.at[pl.ds(i, j - i)], swapped.at[pl.ds(i, j - i)])], sems, len(RUNS) + r)
    finish(leaving)


def swap(heads):
    (swapped,) = call(swap_kernel, [ARRIVED], [ARRIVED], 2 * len(RUNS), (heads,))
    return swapped


def middle_kernel(
    grad_out, third, x_turn, edge, gated, pairs,
    payload_hbm, states_hbm,
    g_cat, states, payload, sems,
):
    row = iota((128, 128), 0)
    col = iota((128, 128), 1)
    token = row.astype(F32)
    total = [jnp.zeros((WIDTH, SPAN), F32) for _ in range(GROUPS)]
    for n in range(SPANS):
        at, here = pl.ds(n * WIDTH, WIDTH), pl.ds(n * SPAN, SPAN)
        y = grad_out[CH_ORDER[n]].astype(F32) * third[:, here].astype(F32)
        hi, lo = high(y), low(y)
        for g in range(GROUPS):
            c = slice(g * WIDTH, (g + 1) * WIDTH)
            g_cat[at, pl.ds(256 * g, 128)] = hi[c]
            g_cat[at, pl.ds(256 * g + 128, 128)] = lo[c]
            total[g] = total[g] + y[c] * gated[at, pl.ds(128 * g, 128)]
    a = edge[WIDTH : WIDTH + 1, :]
    states[...] = halves(dot(g_cat[...], state_matrix(a, token + 1.0)))
    outputs = begin([(states, states_hbm)], sems)
    cross = []
    for g in range(GROUPS):
        four = dot(x_turn[g], g_cat[:, pl.ds(256 * g, 256)])
        four = halves(four[:128] + four[128:])
        four = jnp.where(col >= row, four, 0.0)
        cross += [high(four), low(four)]
    near = halves(dot(jnp.concatenate(cross, axis=1), state_matrix(a, token - 64.0)))
    near = near * jnp.exp(a * (token - 64.0))
    near = jnp.sum(near.reshape(16, 8, 128), axis=0)
    step = jnp.exp(-a * 128.0)
    carry = jnp.zeros((WIDTH, 128), F32)
    far = jnp.zeros((WIDTH, 128), F32)
    odd = iota((WIDTH, 128), 1) >= 64
    for n in reversed(range(0, SPANS, 2)):
        later, earlier = states[pl.ds((n + 1) * WIDTH, WIDTH), :], states[pl.ds(n * WIDTH, WIDTH), :]
        far = far + jnp.where(odd, later, earlier) * pairs[pl.ds(n * WIDTH // 2, WIDTH), :].astype(F32)
        carry = (carry * step + later) * step + earlier
    far = far[:8] + far[8:]
    far = far + pltpu.roll(far, 32, 1)
    weight = near + (far + pltpu.roll(far, 64, 1)) * jnp.exp(a)
    direct = lax.dot_general(
        jnp.ones((8, SPAN), F32),
        jnp.concatenate(total * 4, axis=0),
        (((1,), (1,)), ((), ())),
        precision=lax.Precision.HIGHEST,
        preferred_element_type=F32,
    )
    quarter = iota((8, 128), 1) // 32
    back = jnp.where(
        quarter == 0, carry[:8], jnp.where(quarter == 1, carry[8:], jnp.where(quarter == 2, weight, direct))
    )
    ahead = jnp.where(quarter == 0, edge[0:8, :], edge[8:16, :])
    for k in range(CTX):
        payload[k, :8, :] = back
        payload[k, 8:, :] = ahead
    finish(outputs + begin([(payload, payload_hbm)], sems, 1))


def backward_kernel(
    grad_out, third, states_hbm, back_toep_hbm, mats_hbm, conv_hbm, a_row, skip, place,
    mixed, small, mats, conv,
    g_cat, states, back_toep, leave, sems,
):
    states_in, mats_in, toep_in, conv_in = begin(
        [(states_hbm, states), (mats_hbm, mats), (back_toep_hbm, back_toep), (conv_hbm, conv)], sems
    )
    a = a_row[...]
    wide = jnp.broadcast_to(a, (8, 128)) * float(LENGTH)
    is_state = iota((8, 128), 1) < 64
    me = place[0]
    for k in range(CTX):
        after = jnp.maximum(k - me - 1, 0).astype(F32)
        before = jnp.maximum(me - 1 - k, 0).astype(F32)
        later = jnp.where(k > me, 1.0, 0.0)
        earlier = jnp.where(k < me, 1.0, 0.0)
        small[k] = jnp.where(is_state, jnp.exp(-wide * after) * later, 1.0)
        small[CTX + k] = jnp.exp(-wide * before) * earlier
    small[2 * CTX] = jnp.broadcast_to(a, (8, 128))
    for n in range(SPANS):
        at, here = pl.ds(n * WIDTH, WIDTH), pl.ds(n * SPAN, SPAN)
        y = grad_out[CH_ORDER[n]].astype(F32) * third[:, here].astype(F32)
        hi, lo = high(y), low(y)
        for g in range(GROUPS):
            c = slice(g * WIDTH, (g + 1) * WIDTH)
            g_cat[at, pl.ds(256 * g, 128)] = hi[c]
            g_cat[at, pl.ds(256 * g + 128, 128)] = lo[c]
    lane = iota((WIDTH, 128), 1)
    finish([states_in])
    step = jnp.exp(-a * 128.0)
    carry = jnp.zeros((WIDTH, 128), F32)
    for n in reversed(range(SPANS)):
        at = pl.ds(n * WIDTH, WIDTH)
        leave[at, :] = quad_split(carry, lane)
        carry = carry * step + states[at, :]
    finish([mats_in])
    mixed[...] = dot(leave[...], mats[1])
    finish([toep_in])
    for g in range(GROUPS):
        here = pl.ds(128 * g, 128)
        y = g_cat[:, pl.ds(256 * g, 256)]
        gain = jnp.concatenate([skip[g]] * SPANS, axis=0)
        grad_conv = y[:, :128].astype(F32) + y[:, 128:].astype(F32)
        mixed[:, here] = mixed[:, here] + halves(dot(y, back_toep[g])) + gain * grad_conv
    finish([conv_in])


def finish_kernel(
    parts, small, mats, conv, mixed, grad_out, first_hbm, second_hbm,
    grad_first_hbm, grad_second_hbm, grad_third_hbm, grad_residue_hbm, grad_skip_hbm,
    first, second, grad_first, grad_second, grad_third, grad_residue, grad_skip, decays, left, result,
    sems,
):
    gates_in = begin([(first_hbm, first), (second_hbm, second)], sems)
    a = small[2 * CTX, 0:1, :]
    quarter = iota((8, 128), 1) // 32
    back = jnp.zeros((8, 128), F32)
    ahead = jnp.zeros((8, 128), F32)
    running = jnp.zeros((8, 128), F32)
    far = jnp.zeros((8, 128), F32)
    block_step = jnp.exp(-a * float(LENGTH))
    for k in range(CTX):
        at = CTX_PLACE[k]
        later, earlier = parts[at, :8, :], parts[at, 8:, :]
        back = back + later * small[k]
        ahead = ahead + earlier * small[CTX + k]
        far = far + later * running
        running = running * block_step + earlier

    def spread(x, q):
        x = jnp.where(quarter == q, x, 0.0)
        x = x + pltpu.roll(x, 32, 1)
        return x + pltpu.roll(x, 64, 1)

    def rows(x):
        return jnp.concatenate([spread(x, 0), spread(x, 1)], axis=0)

    span = iota((SPANS, 128), 0).astype(F32)
    decays[0] = jnp.exp(-a * (128.0 * span))
    decays[1] = jnp.exp(-a * (128.0 * (SPANS - 1.0 - span)))
    lane = iota((ROWS, 128), 1)

    def fix(x, side):
        whole = (decays[side].reshape(SPANS, 1, 128) * x.reshape(1, WIDTH, 128)).reshape(ROWS, 128)
        left[...] = quad_split(whole, lane)
        return dot(left[...], mats[side])

    result[...] = conv[...] + fix(rows(ahead), 0)
    outputs = []
    for g in range(GROUPS):
        mine = pl.ds(g * WIDTH, WIDTH)
        for n in range(SPANS):
            full = result[pl.ds(n * WIDTH, WIDTH), pl.ds(128 * g, 128)]
            heads = grad_out[CH_ORDER[n], mine, :].astype(F32)
            grad_third[mine, pl.ds(n * SPAN, SPAN)] = (heads * full).astype(BF16)
        outputs += begin([(grad_third.at[mine, :], grad_third_hbm.at[mine, :])], sems, 2 + g)
    near = spread(back, 2)
    crossed = (spread(far, 0) + spread(far, 1)) * jnp.exp(a)
    weight = jnp.sum(near + crossed, axis=0, keepdims=True)
    weight = weight * jnp.sqrt(2.0 * a) * (1.0 / (float(WIDTH * TOKENS) ** 0.5))
    grad_residue[0:1, :] = weight[:, :MODES]
    grad_residue[1:2, :] = pltpu.roll(weight, 128 - MODES, 1)[:, :MODES]
    direct = pltpu.roll(back, 32, 1)[0:1] * (1.0 / (float(TOKENS) ** 0.5))
    grad_skip[...] = direct[:, : GROUPS * WIDTH]
    outputs += begin([(grad_residue, grad_residue_hbm), (grad_skip, grad_skip_hbm)], sems, 4)
    result[...] = mixed[...] + fix(rows(back), 1)
    finish(gates_in)
    for g in range(GROUPS):
        mine = pl.ds(g * WIDTH, WIDTH)
        for n in range(SPANS):
            here = pl.ds(n * SPAN, SPAN)
            part = result[pl.ds(n * WIDTH, WIDTH), pl.ds(128 * g, 128)]
            grad_first[mine, here] = (part * second[mine, here].astype(F32)).astype(BF16)
            grad_second[mine, here] = (part * first[mine, here].astype(F32)).astype(BF16)
        outputs += begin(
            [
                (grad_first.at[mine, :], grad_first_hbm.at[mine, :]),
                (grad_second.at[mine, :], grad_second_hbm.at[mine, :]),
            ],
            sems,
            6 + 2 * g,
        )
    finish(outputs)


FINISH_COPIES = 10


def placed(kind, shape, dtype):
    return kind(shape, dtype)


def pin(x, kind):
    return pltpu.with_memory_space_constraint(x, kind)


def call(kernel, outs, scratch, copies, args, near=(), vmem=(), smem=(), outs_near=()):
    def space(i):
        return pltpu.VMEM if i in vmem or i in near else pltpu.SMEM if i in smem else pltpu.HBM

    def pinned(i, x):
        return x if i in vmem or i in smem else pin(x, space(i))

    kinds = [pltpu.VMEM if i in outs_near else pltpu.HBM for i in range(len(outs))]
    return pl.pallas_call(
        kernel,
        out_shape=tuple(placed(kind, s, d) for kind, (s, d) in zip(kinds, outs)),
        in_specs=[pl.BlockSpec(memory_space=space(i)) for i in range(len(args))],
        out_specs=tuple(pl.BlockSpec(memory_space=kind) for kind in kinds),
        scratch_shapes=[pltpu.VMEM(s, d) for s, d in scratch]
        + [pltpu.SemaphoreType.DMA((copies,))] * (copies > 0),
        compiler_params=pltpu.CompilerParams(vmem_limit_bytes=40 << 20),
    )(*(pinned(i, x) for i, x in enumerate(args)))


def prepare(residue, decay_rate, skip_gain):
    weight = residue * jnp.sqrt(2.0 * decay_rate)
    a_row = jnp.tile(decay_rate.reshape(1, 32), (1, 4))
    a_col = jnp.tile(decay_rate.reshape(32, 1), (4, 1))
    w_col = jnp.tile(weight.reshape(32, 1), (4, 1))
    return a_row, a_col, w_col, weight, skip_gain.reshape(GROUPS, WIDTH, 1)


GATE = ((GROUPS * WIDTH, LENGTH), BF16)
ARRIVED = ((SPANS, GROUPS * WIDTH, SPAN), BF16)
CAT = ((ROWS, 512), BF16)
TURN = ((GROUPS, 256, ROWS), BF16)
WHOLE = ((ROWS, 256), F32)
STATES = ((ROWS, 128), F32)
ENTER = ((ROWS, 128), BF16)
PAIRS = ((ROWS // 2, 128), BF16)
EDGE = ((WIDTH + 8, 128), F32)
TOEP = ((GROUPS, 256, 256), BF16)
MATS = ((2, 128, 256), BF16)
PARTS = ((CTX, 16, 128), F32)
SMALL = ((2 * CTX + 1, 8, 128), F32)
DECAYS = ((2, SPANS, 128), F32)
RESIDUE = ((GROUPS, MODES), F32)
SKIP = ((1, GROUPS * WIDTH), F32)


def local(first, second, third, grad_out, exchange, residue, decay_rate, skip_gain, place):
    a_row, a_col, w_col, weight, skip = prepare(residue, decay_rate, skip_gain)
    x_turn, edge, third, gated, pairs, conv, back_toep, mats = call(
        forward_kernel,
        [TURN, EDGE, GATE, WHOLE, PAIRS, WHOLE, TOEP, MATS],
        [GATE, GATE, CAT, ENTER, WHOLE, TOEP, MATS, STATES, TOEP],
        6,
        (first, second, third, a_row, a_col, w_col, decay_rate, weight, skip),
        vmem=(3, 4, 5, 8),
        smem=(6, 7),
        outs_near=(0, 1, 2, 3, 4),
    )
    payload, states = call(
        middle_kernel,
        [PARTS, STATES],
        [CAT, STATES, PARTS],
        2,
        (grad_out, third, x_turn, edge, gated, pairs),
        near=(0, 1, 2, 3, 4, 5),
    )
    parts = exchange(payload)
    mixed, small, mats, conv = call(
        backward_kernel,
        [WHOLE, SMALL, MATS, WHOLE],
        [CAT, STATES, TOEP, ENTER],
        4,
        (grad_out, third, states, back_toep, mats, conv, a_row, skip, place),
        near=(0, 1),
        vmem=(6, 7),
        smem=(8,),
        outs_near=(0, 1, 2, 3),
    )
    outs = [GATE, GATE, GATE, RESIDUE, SKIP]
    grad_first, grad_second, grad_third, grad_residue, grad_skip = call(
        finish_kernel,
        outs,
        [GATE, GATE] + outs + [DECAYS, ENTER, WHOLE],
        FINISH_COPIES,
        (parts, small, mats, conv, mixed, grad_out, first, second),
        near=(0, 1, 2, 3, 4, 5),
    )
    return grad_first, grad_second, grad_third, grad_residue, grad_skip.reshape(GROUPS * WIDTH)


def on_device(first, second, third, grad_heads, residue, decay_rate, skip_gain):
    grad_out = lax.all_to_all(
        swap(grad_heads.reshape(SPANS, GROUPS * WIDTH, SPAN)),
        "ch",
        split_axis=0,
        concat_axis=0,
        tiled=True,
        axis_index_groups=[CH_ORDER],
    )
    place = lax.axis_index("ctx").astype(jnp.int32).reshape(1)

    def exchange(payload):
        return lax.all_to_all(
            payload, "ctx", split_axis=0, concat_axis=0, tiled=True, axis_index_groups=[CTX_ORDER]
        )

    return local(first, second, third, grad_out, exchange, residue, decay_rate, skip_gain, place)


def solution(mesh):
    return jax.shard_map(
        on_device,
        mesh=mesh,
        in_specs=(
            P("ch", "ctx"),
            P("ch", "ctx"),
            P("ch", "ctx"),
            P(None, ("ctx", "ch")),
            P("ch", None),
            P("ch", None),
            P("ch"),
        ),
        out_specs=(P("ch", "ctx"), P("ch", "ctx"), P("ch", "ctx"), P("ch", None), P("ch")),
        check_vma=False,
    )
```

```python
import jax
import jax.numpy as jnp
from jax import lax
from jax.experimental import pallas as pl
from jax.experimental.pallas import tpu as pltpu
from jax.sharding import PartitionSpec as P

F32, BF16 = jnp.float32, jnp.bfloat16
SPAN = 128
SPANS = 64
GROUPS, WIDTH, MODES = 2, 16, 16
ROWS = SPANS * WIDTH
LENGTH = SPAN * SPANS
CTX = 8
TOKENS = LENGTH * CTX


def iota(shape, dim):
    return lax.broadcasted_iota(jnp.int32, shape, dim)


def high(x):
    return x.astype(BF16)


def low(x):
    return (x - x.astype(BF16).astype(F32)).astype(BF16)


def dot(a, b):
    return jnp.dot(a, b, preferred_element_type=F32)


def halves(x):
    return x[:, :128] + x[:, 128:]


def state_matrix(a_row, age):
    decay = jnp.exp(-a_row * age)
    lane_group = (iota((128, 128), 1) % 32) // MODES
    out = []
    for g in range(GROUPS):
        mine = jnp.where(lane_group == g, decay, 0.0)
        block = jnp.concatenate([high(mine), low(mine)], axis=1)
        out += [block, block]
    return jnp.concatenate(out, axis=0)


def mode_matrix(a_col, w_col, age):
    wave = w_col * jnp.exp(-a_col * age)
    row = iota((128, 128), 0)
    part = jnp.where(row < 64, wave.astype(BF16).astype(F32), low(wave).astype(F32))
    row_group = (row % 32) // MODES
    return jnp.concatenate(
        [jnp.where(row_group == g, part, 0.0).astype(BF16) for g in range(GROUPS)], axis=1
    )


def quad_split(x, lane):
    top = x.astype(BF16).astype(F32)
    return jnp.where((lane // 32) % 2 == 0, top, x - top).astype(BF16)


def toeplitz(a_s, w_s, g, gap):
    near = jnp.maximum(gap, 0).astype(F32)
    total = jnp.zeros((SPAN, SPAN), F32)
    for r in range(MODES):
        total = total + w_s[g, r] * jnp.exp(-a_s[g, r] * near)
    total = jnp.where(gap >= 0, total, 0.0)
    block = jnp.concatenate([high(total), low(total)], axis=1)
    return jnp.concatenate([block, block], axis=0)


def begin(pairs, sems, first=0):
    copies = [
        pltpu.make_async_copy(source, target, sems.at[first + i]) for i, (source, target) in enumerate(pairs)
    ]
    for copy in copies:
        copy.start()
    return copies


def finish(copies):
    for copy in copies:
        copy.wait()


def forward_kernel(
    first_hbm, second_hbm, third_hbm, a_row, a_col, w_col, a_s, w_s, skip,
    x_turn, edge, third, gated, pairs, conv_hbm, back_toep_hbm, mats_hbm,
    first, second, x_cat, enter, conv, back_toep, mats, states, toep, sems,
):
    inputs = begin([(first_hbm, first), (second_hbm, second)], sems)
    outputs = begin([(third_hbm, third)], sems, 5)
    a = a_row[...]
    row = iota((128, 128), 0)
    col = iota((128, 128), 1)
    token = row.astype(F32)
    lane_token = col.astype(F32)
    mats[0] = mode_matrix(a_col[...], w_col[...], lane_token)
    mats[1] = mode_matrix(a_col[...], w_col[...], 127.0 - lane_token)
    for g in range(GROUPS):
        toep[g] = toeplitz(a_s, w_s, g, col - row)
        back_toep[g] = toeplitz(a_s, w_s, g, row - col)
    outputs += begin([(back_toep, back_toep_hbm), (mats, mats_hbm)], sems, 2)
    finish(inputs)
    for n in range(SPANS):
        at, here = pl.ds(n * WIDTH, WIDTH), pl.ds(n * SPAN, SPAN)
        x = first[:, here].astype(F32) * second[:, here].astype(F32)
        hi, lo = high(x), low(x)
        for g in range(GROUPS):
            c = slice(g * WIDTH, (g + 1) * WIDTH)
            gated[at, pl.ds(128 * g, 128)] = x[c]
            x_cat[at, pl.ds(256 * g, 128)] = hi[c]
            x_cat[at, pl.ds(256 * g + 128, 128)] = lo[c]
    states[...] = halves(dot(x_cat[...], state_matrix(a, 128.0 - token)))
    step = jnp.exp(-a * 128.0)
    carry = jnp.zeros((WIDTH, 128), F32)
    lane = iota((WIDTH, 128), 1)
    for n in range(SPANS):
        at = pl.ds(n * WIDTH, WIDTH)
        enter[at, :] = quad_split(carry, lane)
        carry = carry * step + states[at, :]
    edge[:WIDTH, :] = carry
    edge[WIDTH:, :] = jnp.broadcast_to(a, (8, 128))
    odd = iota((WIDTH, 128), 1) >= 64
    for n in range(0, SPANS, 2):
        even_rows, odd_rows = enter[pl.ds(n * WIDTH, WIDTH), :], enter[pl.ds((n + 1) * WIDTH, WIDTH), :]
        pairs[pl.ds(n * WIDTH // 2, WIDTH), :] = jnp.where(
            odd, odd_rows.astype(F32), even_rows.astype(F32)
        ).astype(BF16)
    conv[...] = dot(enter[...], mats[0])
    for g in range(GROUPS):
        mine = pl.ds(256 * g, 256)
        here = pl.ds(128 * g, 128)
        x = x_cat[:, mine]
        gain = jnp.concatenate([skip[g]] * SPANS, axis=0)
        conv[:, here] = conv[:, here] + halves(dot(x, toep[g])) + gain * gated[:, here]
        x_turn[g] = x.T
    outputs += begin([(conv, conv_hbm)], sems, 4)
    finish(outputs)


FIRST = 45
CH_ORDER = [FIRST if p == 0 else 0 if p == FIRST else p for p in range(SPANS)]
CTX_ORDER = [5, 1, 3, 7, 2, 0, 4, 6]
CTX_PLACE = [CTX_ORDER.index(k) for k in range(CTX)]
RUNS = [(0, 1), (FIRST, FIRST + 1)]
RUNS += [(i, min(i + 22, FIRST)) for i in range(1, FIRST, 22)]
RUNS += [(i, min(i + 22, SPANS)) for i in range(FIRST + 1, SPANS, 22)]


def swap_kernel(heads, swapped, held, sems):
    arriving = begin(
        [(heads.at[pl.ds(CH_ORDER[i], j - i)], held.at[pl.ds(i, j - i)]) for i, j in RUNS], sems
    )
    leaving = []
    for r, (i, j) in enumerate(RUNS):
        finish([arriving[r]])
        leaving += begin([(held.at[pl.ds(i, j - i)], swapped.at[pl.ds(i, j - i)])], sems, len(RUNS) + r)
    finish(leaving)


def swap(heads):
    (swapped,) = call(swap_kernel, [ARRIVED], [ARRIVED], 2 * len(RUNS), (heads,))
    return swapped


def middle_kernel(
    grad_out, third, x_turn, edge, gated, pairs,
    payload_hbm, states_hbm,
    g_cat, states, payload, sems,
):
    row = iota((128, 128), 0)
    col = iota((128, 128), 1)
    token = row.astype(F32)
    total = [jnp.zeros((WIDTH, SPAN), F32) for _ in range(GROUPS)]
    for n in range(SPANS):
        at, here = pl.ds(n * WIDTH, WIDTH), pl.ds(n * SPAN, SPAN)
        y = grad_out[CH_ORDER[n]].astype(F32) * third[:, here].astype(F32)
        hi, lo = high(y), low(y)
        for g in range(GROUPS):
            c = slice(g * WIDTH, (g + 1) * WIDTH)
            g_cat[at, pl.ds(256 * g, 128)] = hi[c]
            g_cat[at, pl.ds(256 * g + 128, 128)] = lo[c]
            total[g] = total[g] + y[c] * gated[at, pl.ds(128 * g, 128)]
    a = edge[WIDTH : WIDTH + 1, :]
    states[...] = halves(dot(g_cat[...], state_matrix(a, token + 1.0)))
    outputs = begin([(states, states_hbm)], sems)
    cross = []
    for g in range(GROUPS):
        four = dot(x_turn[g], g_cat[:, pl.ds(256 * g, 256)])
        four = halves(four[:128] + four[128:])
        four = jnp.where(col >= row, four, 0.0)
        cross += [high(four), low(four)]
    near = halves(dot(jnp.concatenate(cross, axis=1), state_matrix(a, token - 64.0)))
    near = near * jnp.exp(a * (token - 64.0))
    near = jnp.sum(near.reshape(16, 8, 128), axis=0)
    step = jnp.exp(-a * 128.0)
    carry = jnp.zeros((WIDTH, 128), F32)
    far = jnp.zeros((WIDTH, 128), F32)
    odd = iota((WIDTH, 128), 1) >= 64
    for n in reversed(range(0, SPANS, 2)):
        later, earlier = states[pl.ds((n + 1) * WIDTH, WIDTH), :], states[pl.ds(n * WIDTH, WIDTH), :]
        far = far + jnp.where(odd, later, earlier) * pairs[pl.ds(n * WIDTH // 2, WIDTH), :].astype(F32)
        carry = (carry * step + later) * step + earlier
    far = far[:8] + far[8:]
    far = far + pltpu.roll(far, 32, 1)
    weight = near + (far + pltpu.roll(far, 64, 1)) * jnp.exp(a)
    sums = jnp.concatenate(total * 4, axis=0)
    direct = lax.dot_general(
        jnp.ones((8, 2 * SPAN), BF16),
        jnp.concatenate([high(sums), low(sums)], axis=1),
        (((1,), (1,)), ((), ())),
        preferred_element_type=F32,
    )
    quarter = iota((8, 128), 1) // 32
    back = jnp.where(
        quarter == 0, carry[:8], jnp.where(quarter == 1, carry[8:], jnp.where(quarter == 2, weight, direct))
    )
    ahead = jnp.where(quarter == 0, edge[0:8, :], edge[8:16, :])
    for k in range(CTX):
        payload[k, :8, :] = back
        payload[k, 8:, :] = ahead
    finish(outputs + begin([(payload, payload_hbm)], sems, 1))


def backward_kernel(
    grad_out, third, states_hbm, back_toep_hbm, mats_hbm, conv_hbm, a_row, skip, place,
    mixed, small, mats, conv,
    g_cat, states, back_toep, leave, sems,
):
    states_in, mats_in, toep_in, conv_in = begin(
        [(states_hbm, states), (mats_hbm, mats), (back_toep_hbm, back_toep), (conv_hbm, conv)], sems
    )
    a = a_row[...]
    wide = jnp.broadcast_to(a, (8, 128)) * float(LENGTH)
    is_state = iota((8, 128), 1) < 64
    me = place[0]
    for k in range(CTX):
        after = jnp.maximum(k - me - 1, 0).astype(F32)
        before = jnp.maximum(me - 1 - k, 0).astype(F32)
        later = jnp.where(k > me, 1.0, 0.0)
        earlier = jnp.where(k < me, 1.0, 0.0)
        small[k] = jnp.where(is_state, jnp.exp(-wide * after) * later, 1.0)
        small[CTX + k] = jnp.exp(-wide * before) * earlier
    small[2 * CTX] = jnp.broadcast_to(a, (8, 128))
    for n in range(SPANS):
        at, here = pl.ds(n * WIDTH, WIDTH), pl.ds(n * SPAN, SPAN)
        y = grad_out[CH_ORDER[n]].astype(F32) * third[:, here].astype(F32)
        hi, lo = high(y), low(y)
        for g in range(GROUPS):
            c = slice(g * WIDTH, (g + 1) * WIDTH)
            g_cat[at, pl.ds(256 * g, 128)] = hi[c]
            g_cat[at, pl.ds(256 * g + 128, 128)] = lo[c]
    lane = iota((WIDTH, 128), 1)
    finish([states_in])
    step = jnp.exp(-a * 128.0)
    carry = jnp.zeros((WIDTH, 128), F32)
    for n in reversed(range(SPANS)):
        at = pl.ds(n * WIDTH, WIDTH)
        leave[at, :] = quad_split(carry, lane)
        carry = carry * step + states[at, :]
    finish([mats_in])
    mixed[...] = dot(leave[...], mats[1])
    finish([toep_in])
    for g in range(GROUPS):
        here = pl.ds(128 * g, 128)
        y = g_cat[:, pl.ds(256 * g, 256)]
        gain = jnp.concatenate([skip[g]] * SPANS, axis=0)
        grad_conv = y[:, :128].astype(F32) + y[:, 128:].astype(F32)
        mixed[:, here] = mixed[:, here] + halves(dot(y, back_toep[g])) + gain * grad_conv
    finish([conv_in])


def finish_kernel(
    parts, small, mats, conv, mixed, grad_out, first_hbm, second_hbm,
    grad_first_hbm, grad_second_hbm, grad_third_hbm, grad_residue_hbm, grad_skip_hbm,
    first, second, grad_first, grad_second, grad_third, grad_residue, grad_skip, decays, left, result,
    sems,
):
    gates_in = begin([(first_hbm, first), (second_hbm, second)], sems)
    a = small[2 * CTX, 0:1, :]
    quarter = iota((8, 128), 1) // 32
    back = jnp.zeros((8, 128), F32)
    ahead = jnp.zeros((8, 128), F32)
    running = jnp.zeros((8, 128), F32)
    far = jnp.zeros((8, 128), F32)
    block_step = jnp.exp(-a * float(LENGTH))
    for k in range(CTX):
        at = CTX_PLACE[k]
        later, earlier = parts[at, :8, :], parts[at, 8:, :]
        back = back + later * small[k]
        ahead = ahead + earlier * small[CTX + k]
        far = far + later * running
        running = running * block_step + earlier

    def spread(x, q):
        x = jnp.where(quarter == q, x, 0.0)
        x = x + pltpu.roll(x, 32, 1)
        return x + pltpu.roll(x, 64, 1)

    def rows(x):
        return jnp.concatenate([spread(x, 0), spread(x, 1)], axis=0)

    span = iota((SPANS, 128), 0).astype(F32)
    decays[0] = jnp.exp(-a * (128.0 * span))
    decays[1] = jnp.exp(-a * (128.0 * (SPANS - 1.0 - span)))
    lane = iota((ROWS, 128), 1)

    def fix(x, side):
        whole = (decays[side].reshape(SPANS, 1, 128) * x.reshape(1, WIDTH, 128)).reshape(ROWS, 128)
        left[...] = quad_split(whole, lane)
        return dot(left[...], mats[side])

    result[...] = conv[...] + fix(rows(ahead), 0)
    outputs = []
    for g in range(GROUPS):
        mine = pl.ds(g * WIDTH, WIDTH)
        for n in range(SPANS):
            full = result[pl.ds(n * WIDTH, WIDTH), pl.ds(128 * g, 128)]
            heads = grad_out[CH_ORDER[n], mine, :].astype(F32)
            grad_third[mine, pl.ds(n * SPAN, SPAN)] = (heads * full).astype(BF16)
        outputs += begin([(grad_third.at[mine, :], grad_third_hbm.at[mine, :])], sems, 2 + g)
    near = spread(back, 2)
    crossed = (spread(far, 0) + spread(far, 1)) * jnp.exp(a)
    weight = jnp.sum(near + crossed, axis=0, keepdims=True)
    weight = weight * jnp.sqrt(2.0 * a) * (1.0 / (float(WIDTH * TOKENS) ** 0.5))
    grad_residue[0:1, :] = weight[:, :MODES]
    grad_residue[1:2, :] = pltpu.roll(weight, 128 - MODES, 1)[:, :MODES]
    direct = pltpu.roll(back, 32, 1)[0:1] * (1.0 / (float(TOKENS) ** 0.5))
    grad_skip[...] = direct[:, : GROUPS * WIDTH]
    outputs += begin([(grad_residue, grad_residue_hbm), (grad_skip, grad_skip_hbm)], sems, 4)
    result[...] = mixed[...] + fix(rows(back), 1)
    finish(gates_in)
    for g in range(GROUPS):
        mine = pl.ds(g * WIDTH, WIDTH)
        for n in range(SPANS):
            here = pl.ds(n * SPAN, SPAN)
            part = result[pl.ds(n * WIDTH, WIDTH), pl.ds(128 * g, 128)]
            grad_first[mine, here] = (part * second[mine, here].astype(F32)).astype(BF16)
            grad_second[mine, here] = (part * first[mine, here].astype(F32)).astype(BF16)
        outputs += begin(
            [
                (grad_first.at[mine, :], grad_first_hbm.at[mine, :]),
                (grad_second.at[mine, :], grad_second_hbm.at[mine, :]),
            ],
            sems,
            6 + 2 * g,
        )
    finish(outputs)


FINISH_COPIES = 10


def placed(kind, shape, dtype):
    return kind(shape, dtype)


def pin(x, kind):
    return pltpu.with_memory_space_constraint(x, kind)


def call(kernel, outs, scratch, copies, args, near=(), vmem=(), smem=(), outs_near=()):
    def space(i):
        return pltpu.VMEM if i in vmem or i in near else pltpu.SMEM if i in smem else pltpu.HBM

    def pinned(i, x):
        return x if i in vmem or i in smem else pin(x, space(i))

    kinds = [pltpu.VMEM if i in outs_near else pltpu.HBM for i in range(len(outs))]
    return pl.pallas_call(
        kernel,
        out_shape=tuple(placed(kind, s, d) for kind, (s, d) in zip(kinds, outs)),
        in_specs=[pl.BlockSpec(memory_space=space(i)) for i in range(len(args))],
        out_specs=tuple(pl.BlockSpec(memory_space=kind) for kind in kinds),
        scratch_shapes=[pltpu.VMEM(s, d) for s, d in scratch]
        + [pltpu.SemaphoreType.DMA((copies,))] * (copies > 0),
        compiler_params=pltpu.CompilerParams(vmem_limit_bytes=40 << 20),
    )(*(pinned(i, x) for i, x in enumerate(args)))


def prepare(residue, decay_rate, skip_gain):
    weight = residue * jnp.sqrt(2.0 * decay_rate)
    a_row = jnp.tile(decay_rate.reshape(1, 32), (1, 4))
    a_col = jnp.tile(decay_rate.reshape(32, 1), (4, 1))
    w_col = jnp.tile(weight.reshape(32, 1), (4, 1))
    return a_row, a_col, w_col, weight, skip_gain.reshape(GROUPS, WIDTH, 1)


GATE = ((GROUPS * WIDTH, LENGTH), BF16)
ARRIVED = ((SPANS, GROUPS * WIDTH, SPAN), BF16)
CAT = ((ROWS, 512), BF16)
TURN = ((GROUPS, 256, ROWS), BF16)
WHOLE = ((ROWS, 256), F32)
STATES = ((ROWS, 128), F32)
ENTER = ((ROWS, 128), BF16)
PAIRS = ((ROWS // 2, 128), BF16)
EDGE = ((WIDTH + 8, 128), F32)
TOEP = ((GROUPS, 256, 256), BF16)
MATS = ((2, 128, 256), BF16)
PARTS = ((CTX, 16, 128), F32)
SMALL = ((2 * CTX + 1, 8, 128), F32)
DECAYS = ((2, SPANS, 128), F32)
RESIDUE = ((GROUPS, MODES), F32)
SKIP = ((1, GROUPS * WIDTH), F32)


def local(first, second, third, grad_out, exchange, residue, decay_rate, skip_gain, place):
    a_row, a_col, w_col, weight, skip = prepare(residue, decay_rate, skip_gain)
    x_turn, edge, third, gated, pairs, conv, back_toep, mats = call(
        forward_kernel,
        [TURN, EDGE, GATE, WHOLE, PAIRS, WHOLE, TOEP, MATS],
        [GATE, GATE, CAT, ENTER, WHOLE, TOEP, MATS, STATES, TOEP],
        6,
        (first, second, third, a_row, a_col, w_col, decay_rate, weight, skip),
        vmem=(3, 4, 5, 8),
        smem=(6, 7),
        outs_near=(0, 1, 2, 3, 4),
    )
    payload, states = call(
        middle_kernel,
        [PARTS, STATES],
        [CAT, STATES, PARTS],
        2,
        (grad_out, third, x_turn, edge, gated, pairs),
        near=(0, 1, 2, 3, 4, 5),
    )
    parts = exchange(payload)
    mixed, small, mats, conv = call(
        backward_kernel,
        [WHOLE, SMALL, MATS, WHOLE],
        [CAT, STATES, TOEP, ENTER],
        4,
        (grad_out, third, states, back_toep, mats, conv, a_row, skip, place),
        near=(0, 1),
        vmem=(6, 7),
        smem=(8,),
        outs_near=(0, 1, 2, 3),
    )
    outs = [GATE, GATE, GATE, RESIDUE, SKIP]
    grad_first, grad_second, grad_third, grad_residue, grad_skip = call(
        finish_kernel,
        outs,
        [GATE, GATE] + outs + [DECAYS, ENTER, WHOLE],
        FINISH_COPIES,
        (parts, small, mats, conv, mixed, grad_out, first, second),
        near=(0, 1, 2, 3, 4, 5),
    )
    return grad_first, grad_second, grad_third, grad_residue, grad_skip.reshape(GROUPS * WIDTH)


def on_device(first, second, third, grad_heads, residue, decay_rate, skip_gain):
    grad_out = lax.all_to_all(
        swap(grad_heads.reshape(SPANS, GROUPS * WIDTH, SPAN)),
        "ch",
        split_axis=0,
        concat_axis=0,
        tiled=True,
        axis_index_groups=[CH_ORDER],
    )
    place = lax.axis_index("ctx").astype(jnp.int32).reshape(1)

    def exchange(payload):
        return lax.all_to_all(
            payload, "ctx", split_axis=0, concat_axis=0, tiled=True, axis_index_groups=[CTX_ORDER]
        )

    return local(first, second, third, grad_out, exchange, residue, decay_rate, skip_gain, place)


def solution(mesh):
    return jax.shard_map(
        on_device,
        mesh=mesh,
        in_specs=(
            P("ch", "ctx"),
            P("ch", "ctx"),
            P("ch", "ctx"),
            P(None, ("ctx", "ch")),
            P("ch", None),
            P("ch", None),
            P("ch"),
        ),
        out_specs=(P("ch", "ctx"), P("ch", "ctx"), P("ch", "ctx"), P("ch", None), P("ch")),
        check_vma=False,
    )
```
